512 devices in a mesh: mem: 16 (over z), lat: 32 (over x, y, core).
Axes of the slice: x: 4, y: 4, z: 16, core: 2. Of those that a mesh axis runs over, the one named last changes fastest.
Arguments:
- perturbation: bfloat16 [16, 160, 320, 128], P('mem', 'lat'), may hold values from -30 to 30
- owner_map: int32 [160], replicated, may hold values from 0 to 159, each once
- band_widths: int32 [16], replicated, may hold values from 1 to 20, 160 in all
Outputs:
- whitened: bfloat16 [16, 2, 160, 160, 128], P('mem', None, 'lat')
- inverse_root: float32 [16, 128, 128], replicated
The draws below stay inside these ranges and needn't reach their ends.
Inputs may be any that keep to these rules, and one draw needn't show every extreme that they name: `owner_map`: each zonal wavenumber 0 to 159 stands at exactly one position. `band_widths`: the widths sum to 160; the widest band holds exactly 20 total wavenumbers.
All inputs are finite; a program needn't handle non-finite values.
Results may differ from the reference program's by a relative error of at most 0.0024.
The reference program's roundings to bfloat16 on the way count: a program that leaves them out, or rounds other values in their place, can miss the bound.
Values may be sent and summed in bfloat16 or wider, within the bound.
A program may use at most 64 MiB of HBM per device.

```python
import math
import jax
import jax.numpy as jnp
import numpy as np
from jax import lax

NLAT = 160
NLON = 320
MM = 160
LEVELS = 128
BANDS = 16
MOST = 20
NS_ITERS = 6
MEMBERS = 16


def draw_perturbation(key, part):
    key_level = jax.random.fold_in(jax.random.fold_in(key, 11), 0)
    key_noise = jax.random.fold_in(jax.random.fold_in(key, 11), 1)
    key_phase = jax.random.fold_in(jax.random.fold_in(key, 11), 4)
    level_scale = jnp.exp(jax.random.uniform(key_level, (LEVELS,), jnp.float32, jnp.log(0.3), jnp.log(3.0)))
    grid_shape = (MEMBERS, NLAT, NLON, LEVELS)
    random_part = jax.random.normal(key_noise, grid_shape, jnp.float32)
    blended = random_part + 0.6 * jnp.roll(random_part, 1, axis=3) + 0.3 * jnp.roll(random_part, 2, axis=3)
    member_index = jnp.arange(MEMBERS, dtype=jnp.int32)[:, None, None, None]
    level_index = jnp.arange(LEVELS, dtype=jnp.int32)[None, None, None, :]
    own_levels = level_index * MEMBERS // LEVELS == member_index
    longitude = jnp.arange(NLON, dtype=jnp.float32)[None, None, :, None]
    colatitude = (jnp.pi * (jnp.arange(NLAT, dtype=jnp.float32) + 0.5) / NLAT)[None, :, None, None]
    phase = jax.random.uniform(key_phase, (MEMBERS, 1, 1, LEVELS), jnp.float32, -jnp.pi, jnp.pi)
    planetary = jnp.where(own_levels, 4.0, 0.0) * (1.0 + 0.5 * jnp.cos(3.0 * colatitude)) * jnp.cos(2.0 * jnp.pi * longitude / NLON + phase)
    return jnp.clip((blended + planetary) * level_scale, -30.0, 30.0).astype(jnp.bfloat16)


def length_profile(amount, total, limit, slope):
    weights = [(1 << 20) // math.isqrt(grade ** slope) + 1 for grade in range(2, amount + 1)]
    surplus, holding = total - limit - (amount - 1), [1] * (amount - 1)
    while surplus > 0:
        free = [i for i in range(amount - 1) if holding[i] < limit]
        whole, left = sum([weights[i] for i in free]), surplus
        for i in free:
            more = min(limit - holding[i], max(1, left * weights[i] // whole), surplus)
            holding[i] = holding[i] + more
            surplus = surplus - more
    return np.array([limit] + holding)


def uneven_parts(key, count, total, most, skew):
    if count == 2:
        one = jax.random.randint(key, (), max(1, total - most), min(most, total - 1) + 1)
        return jnp.stack([one, total - one])
    lengths = jnp.asarray(length_profile(count, total, most, skew), jnp.int32)
    couples = (count - 1) // 2
    donor, taker = lengths[1:1 + 2 * couples:2], lengths[2:2 + 2 * couples:2]
    margin = jnp.minimum(donor - 1, most - taker)
    passed = jax.random.randint(jax.random.fold_in(key, 1), (couples,), 0, 1 << 20) % (margin + 1)
    lengths = lengths.at[1:1 + 2 * couples:2].set(donor - passed).at[2:2 + 2 * couples:2].set(taker + passed)
    return lengths[jax.random.permutation(jax.random.fold_in(key, 2), count)]


def setup_inputs(seed: int = 0) -> dict:
    streams_of = jax.random.split(jax.random.key(seed), 4)
    perturbation = draw_perturbation(jax.random.fold_in(streams_of[3], 71), 0)
    owner_map = jax.random.permutation(streams_of[1], MM).astype(jnp.int32)
    band_widths = uneven_parts(streams_of[2], BANDS, MM, MOST, 1).astype(jnp.int32)
    return dict(perturbation=perturbation, owner_map=owner_map, band_widths=band_widths)


shrink_weight = 0.2

def colatitudes(lat_count):
    position = jnp.arange(lat_count, dtype=jnp.float32)
    colatitude = jnp.pi * (position + 0.5) / lat_count
    return (jnp.cos(colatitude), jnp.sin(colatitude))

def legendre_table(zonal_orders, total_orders, lat_count):
    cosine, sine_row = colatitudes(lat_count)
    counter = jnp.arange(1, total_orders + 1, dtype=jnp.float32)
    log_ratio = jnp.log((2.0 * counter - 1.0) / (2.0 * counter))
    log_factor = lax.optimization_barrier(jnp.sum(jnp.where(counter[None, :] <= zonal_orders[:, None], log_ratio[None, :], 0.0), axis=1))
    log_norm = 0.5 * jnp.log((2.0 * zonal_orders + 1.0) / 2.0) + 0.5 * log_factor
    start_value = jnp.exp(log_norm[:, None] + zonal_orders[:, None] * jnp.log(sine_row)[None, :])
    weights = jnp.sqrt(jnp.pi / lat_count) * sine_row
    zonal = zonal_orders[:, None]

    def advance(state_pair, degree):
        previous, earlier = state_pair
        is_above = degree > zonal
        upper_coef = jnp.sqrt(jnp.maximum(4.0 * degree * degree - 1.0, 1.0) / jnp.where(is_above, degree * degree - zonal * zonal, 1.0))
        lower_degree = degree - 1.0
        lower_coef = jnp.sqrt(jnp.maximum(lower_degree * lower_degree - zonal * zonal, 0.0) / jnp.maximum(4.0 * lower_degree * lower_degree - 1.0, 1.0))
        climbed = upper_coef * (cosine[None, :] * previous - lower_coef * earlier)
        current = jnp.where(is_above, climbed, jnp.where(degree == zonal, start_value, 0.0))
        return ((current, previous), current * weights[None, :])
    zero_rows = jnp.zeros((zonal_orders.shape[0], lat_count), jnp.float32)
    unused_state, poly_table = lax.scan(advance, (zero_rows, zero_rows), jnp.arange(total_orders, dtype=jnp.float32))
    return poly_table

def fourier_table(orders, lon_count):
    longitude = jnp.arange(lon_count, dtype=jnp.int32)
    phases = orders[:, None] * longitude[None, :] % lon_count
    angles = phases.astype(jnp.float32) * (2.0 * jnp.pi / lon_count)
    scaling = jnp.sqrt(2.0 / lon_count)
    return jnp.stack([scaling * jnp.cos(angles), -scaling * jnp.sin(angles)])

def band_rows(band_widths):
    band_end = jnp.cumsum(band_widths).astype(jnp.int32)
    band_start = band_end - band_widths
    lowest = jnp.minimum(band_start, MM - MOST)
    slot_rows = lowest[:, None] + jnp.arange(MOST, dtype=jnp.int32)[None, :]
    band_keep = (slot_rows >= band_start[:, None]) & (slot_rows < band_end[:, None])
    return (band_start, band_end, slot_rows, band_keep)

def inverse_roots(gram, band_start, band_end, member_total):
    band_span = (band_end * band_end - band_start * band_start).astype(jnp.float32)
    covariance = gram / ((member_total - 1.0) * band_span)[:, None, None]
    identity = jnp.eye(LEVELS, dtype=jnp.float32)
    spread = jnp.trace(covariance, axis1=1, axis2=2) / LEVELS
    shrunk = (1.0 - shrink_weight) * covariance + shrink_weight * spread[:, None, None] * identity
    frobenius = jnp.sqrt(lax.optimization_barrier(jnp.sum(shrunk * shrunk, axis=(1, 2))) + 1e-06)
    growing = shrunk / frobenius[:, None, None]
    inverse = jnp.broadcast_to(identity, shrunk.shape)
    for iteration in range(NS_ITERS):
        middle = 1.5 * identity - 0.5 * jnp.matmul(inverse, growing, precision=lax.Precision.HIGHEST)
        growing = jnp.matmul(growing, middle, precision=lax.Precision.HIGHEST)
        inverse = jnp.matmul(middle, inverse, precision=lax.Precision.HIGHEST)
    return inverse / jnp.sqrt(frobenius)[:, None, None]

def reference(perturbation, owner_map, band_widths):
    wave_table = lax.optimization_barrier(fourier_table(owner_map, NLON).astype(jnp.bfloat16)).astype(jnp.float32)
    poly_table = lax.optimization_barrier(legendre_table(owner_map.astype(jnp.float32), MM, NLAT).astype(jnp.bfloat16)).astype(jnp.float32)
    band_start, band_end, slot_rows, band_keep = band_rows(band_widths)
    flat_rows = slot_rows.reshape(-1)
    keep_float = band_keep.astype(jnp.float32)

    def spectral(grid_field):
        grid_wide = grid_field.astype(jnp.float32)
        waves = jnp.einsum('rpk,jkl->rpjl', wave_table, grid_wide)
        waves = lax.optimization_barrier(waves.astype(jnp.bfloat16)).astype(jnp.float32)
        coeffs = jnp.einsum('npj,rpjl->rpnl', poly_table, waves)
        coeffs = lax.optimization_barrier(coeffs.astype(jnp.bfloat16)).astype(jnp.float32)
        picked = jnp.take(coeffs, flat_rows, axis=2).reshape(2, MM, BANDS, MOST, LEVELS)
        return picked * keep_float[None, None, :, :, None]

    def accumulate(gram, grid_field):
        masked = spectral(grid_field)
        return (gram + jnp.einsum('rpbtk,rpbtl->bkl', masked, masked), None)
    gram, unused_out = lax.scan(accumulate, jnp.zeros((BANDS, LEVELS, LEVELS), jnp.float32), perturbation)
    inverse_root = inverse_roots(gram, band_start, band_end, MEMBERS)
    root_low = lax.optimization_barrier(inverse_root.astype(jnp.bfloat16)).astype(jnp.float32)

    def whiten(grid_field):
        masked = spectral(grid_field)
        moved = jnp.einsum('rpbtk,blk->rpbtl', masked, root_low).reshape(2, MM, BANDS * MOST, LEVELS)
        whitened = jnp.zeros((2, MM, MM, LEVELS), jnp.float32).at[:, :, flat_rows, :].add(moved)
        return whitened.astype(jnp.bfloat16)
    return (lax.map(whiten, perturbation), inverse_root)
```

```python
import functools

import jax
import jax.numpy as jnp
import numpy as np
from jax import lax
from jax.experimental import pallas as pl
from jax.experimental.pallas import tpu as pltpu
from jax.sharding import PartitionSpec as P

NLAT = 160
NLON = 320
MM = 160
LEVELS = 128
BANDS = 16
MOST = 20
NS_ITERS = 6

shrink_weight = 0.2


def legendre_kernel(lat_count, zonal_ref, start_ref, cosine_ref, weight_ref, out_ref, rows_ref):
    zonal = zonal_ref[...]
    zonal_square = zonal * zonal
    lanes = start_ref.shape[1] // 128
    start = [start_ref[:, 128 * c : 128 * (c + 1)] for c in range(lanes)]
    cosine = [cosine_ref[:, 128 * c : 128 * (c + 1)] for c in range(lanes)]
    weight = [weight_ref[:, 128 * c : 128 * (c + 1)] for c in range(lanes)]

    def advance(step, carry):
        for inner in range(8):
            index = step * 8 + inner
            degree = index.astype(jnp.float32)
            is_above = degree > zonal
            is_equal = degree == zonal
            upper_coef = jnp.sqrt(
                jnp.maximum(4.0 * degree * degree - 1.0, 1.0)
                / jnp.where(is_above, degree * degree - zonal_square, 1.0)
            )
            lower = degree - 1.0
            lower_coef = jnp.sqrt(
                jnp.maximum(lower * lower - zonal_square, 0.0)
                / jnp.maximum(4.0 * lower * lower - 1.0, 1.0)
            )
            following = []
            for c in range(lanes):
                previous, earlier = carry[2 * c], carry[2 * c + 1]
                climbed = upper_coef * (cosine[c] * previous - lower_coef * earlier)
                current = jnp.where(is_above, climbed, jnp.where(is_equal, start[c], 0.0))
                rows_ref[index, :, 128 * c : 128 * (c + 1)] = current * weight[c]
                following += [current, previous]
            carry = tuple(following)
        return carry

    zero = jnp.zeros_like(zonal)
    lax.fori_loop(0, MM // 8, advance, (zero,) * (2 * lanes))
    for q in range(out_ref.shape[0]):
        out_ref[q] = rows_ref[:, q, :][:, :lat_count].astype(jnp.bfloat16)


def legendre_table(zonal_orders, lat_count):
    owned = zonal_orders.shape[0]
    rows, lanes = 8, (lat_count + 127) // 128 * 128
    colatitude = np.pi * (np.arange(lat_count) + 0.5) / lat_count
    counter = np.arange(1, MM + 1)
    log_ratio = np.log((2.0 * counter - 1.0) / (2.0 * counter)).astype(np.float32)
    log_sine = np.log(np.sin(colatitude)).astype(np.float32)

    def spread(row):
        return np.tile(np.pad(row, (0, lanes - lat_count)).astype(np.float32), (rows, 1))

    cosine = spread(np.cos(colatitude))
    weight = spread(np.sqrt(np.pi / lat_count) * np.sin(colatitude))
    log_factor = jnp.sum(
        jnp.where(counter[None, :] <= zonal_orders[:, None], log_ratio[None, :], 0.0), axis=1
    )
    log_norm = 0.5 * jnp.log((2.0 * zonal_orders + 1.0) / 2.0) + 0.5 * log_factor
    start = jnp.exp(log_norm[:, None] + zonal_orders[:, None] * log_sine[None, :])
    start = jnp.pad(start, ((0, rows - owned), (0, lanes - lat_count)))
    zonal = jnp.broadcast_to(jnp.pad(zonal_orders, (0, rows - owned))[:, None], (rows, 128))
    return pl.pallas_call(
        functools.partial(legendre_kernel, lat_count),
        out_shape=jax.ShapeDtypeStruct((owned, MM, lat_count), jnp.bfloat16),
        in_specs=[pl.BlockSpec(memory_space=pltpu.VMEM)] * 4,
        out_specs=pl.BlockSpec(memory_space=pltpu.VMEM),
        scratch_shapes=[pltpu.VMEM((MM, rows, lanes), jnp.float32)],
        cost_estimate=pl.CostEstimate(
            flops=40_000_000, bytes_accessed=20_000_000, transcendentals=1_000_000
        ),
    )(zonal, start, cosine, weight)


def fourier_table(orders, lon_count):
    phases = np.arange(MM)[:, None] * np.arange(lon_count)[None, :] % lon_count
    angles = phases * (2.0 * np.pi / lon_count)
    scaling = np.sqrt(2.0 / lon_count)
    waves = np.stack([scaling * np.cos(angles), -scaling * np.sin(angles)])
    waves = jnp.asarray(waves.astype(np.float32)).astype(jnp.bfloat16)
    pick = (orders[:, None] == jnp.arange(MM, dtype=jnp.int32)[None, :]).astype(jnp.bfloat16)
    return jnp.einsum(
        "pm,rmk->rpk", pick, waves, preferred_element_type=jnp.float32
    ).astype(jnp.bfloat16)


def band_rows(band_widths):
    band_end = jnp.cumsum(band_widths)
    band_start = band_end - band_widths
    lowest = jnp.minimum(band_start, MM - MOST)
    slot_rows = lowest[:, None] + jnp.arange(MOST, dtype=jnp.int32)[None, :]
    band_keep = (slot_rows >= band_start[:, None]) & (slot_rows < band_end[:, None])
    return (band_start, band_end, slot_rows, band_keep)


def inverse_roots(gram, band_start, band_end, member_total):
    band_span = (band_end * band_end - band_start * band_start).astype(jnp.float32)
    covariance = gram / ((member_total - 1.0) * band_span)[:, None, None]
    identity = jnp.eye(LEVELS, dtype=jnp.float32)
    spread = jnp.trace(covariance, axis1=1, axis2=2) / LEVELS
    shrunk = (1.0 - shrink_weight) * covariance + shrink_weight * spread[:, None, None] * identity
    frobenius = jnp.sqrt(jnp.sum(shrunk * shrunk, axis=(1, 2)) + 1e-06)
    growing = shrunk / frobenius[:, None, None]
    inverse = jnp.broadcast_to(identity, shrunk.shape)
    for iteration in range(NS_ITERS):
        middle = 1.5 * identity - 0.5 * jnp.matmul(
            inverse, growing, precision=lax.Precision.HIGHEST
        )
        growing = jnp.matmul(growing, middle, precision=lax.Precision.HIGHEST)
        inverse = jnp.matmul(middle, inverse, precision=lax.Precision.HIGHEST)
    return inverse / jnp.sqrt(frobenius)[:, None, None]


def reduced_band(partial_gram):
    pieces = lax.axis_size("lat")
    half = BANDS * LEVELS // pieces
    members = lax.axis_size("mem")
    thin = half // members
    chunks = lax.all_to_all(
        partial_gram.reshape(pieces, half, LEVELS), "lat", split_axis=0, concat_axis=0, tiled=True
    )
    own = jnp.sum(chunks, axis=0).reshape(members, thin, LEVELS)
    slices = lax.all_to_all(own, "mem", split_axis=0, concat_axis=0, tiled=True)
    total = jnp.sum(slices, axis=0)
    copies = jnp.broadcast_to(total[None], (members, thin, LEVELS))
    mine = lax.all_to_all(copies, "mem", split_axis=0, concat_axis=0, tiled=True)
    mine = mine.reshape(half, LEVELS)
    other = lax.ppermute(mine, "lat", [(d, d ^ 1) for d in range(pieces)])
    first = lax.axis_index("lat") % 2 == 0
    return jnp.where(
        first, jnp.concatenate([mine, other], axis=0), jnp.concatenate([other, mine], axis=0)
    )


def body(perturbation, owner_map, band_widths):
    members = perturbation.shape[0]
    lat_rows = perturbation.shape[1]
    lat_devices = lax.axis_size("lat")
    lat_index = lax.axis_index("lat")
    owned_count = MM // lat_devices
    wave_table = fourier_table(owner_map, NLON)
    waves = jnp.einsum(
        "rpk,ajkl->arpjl", wave_table, perturbation, preferred_element_type=jnp.float32
    ).astype(jnp.bfloat16)
    owned_waves = lax.dynamic_slice_in_dim(owner_map, lat_index * owned_count, owned_count, 0)
    poly_table = legendre_table(owned_waves.astype(jnp.float32), lat_rows * lat_devices)
    spectral = jnp.einsum(
        "qnj,arqjl->arqnl",
        poly_table,
        lax.all_to_all(waves, "lat", split_axis=2, concat_axis=3, tiled=True),
        preferred_element_type=jnp.float32,
    ).astype(jnp.bfloat16)
    band_start, band_end, slot_rows, band_keep = band_rows(band_widths)
    row_index = jnp.arange(MM, dtype=jnp.int32)
    selector = (row_index[:, None] == slot_rows.reshape(-1)[None, :]) & band_keep.reshape(-1)[
        None, :
    ]
    select_low = selector.astype(jnp.bfloat16)
    masked = jnp.einsum(
        "arqnl,ns->arqsl", spectral, select_low, preferred_element_type=jnp.float32
    ).astype(jnp.bfloat16)
    masked = masked.reshape(members, 2, owned_count, BANDS, MOST, LEVELS)
    partial_gram = jnp.einsum(
        "arqbtk,arqbtl->bkl", masked, masked, preferred_element_type=jnp.float32
    )
    member_total = members * lax.axis_size("mem")
    bands_here = lax.axis_size("lat") // BANDS
    band = lat_index // bands_here
    gram = reduced_band(partial_gram)
    own_start = lax.dynamic_slice_in_dim(band_start, band, 1, 0)
    own_end = lax.dynamic_slice_in_dim(band_end, band, 1, 0)
    own_root = inverse_roots(gram[None], own_start, own_end, member_total)[0]
    half = LEVELS // bands_here
    own_half = lax.dynamic_slice_in_dim(own_root, (lat_index % bands_here) * half, half, 0)
    copies = jnp.broadcast_to(own_half[None], (lat_devices, half, LEVELS))
    inverse_root = lax.all_to_all(copies, "lat", split_axis=0, concat_axis=0, tiled=True)
    inverse_root = inverse_root.reshape(BANDS, LEVELS, LEVELS)
    root_low = inverse_root.astype(jnp.bfloat16)
    moved = jnp.einsum("arqbtk,blk->arqbtl", masked, root_low, preferred_element_type=jnp.float32)
    moved = moved.astype(jnp.bfloat16).reshape(members, 2, owned_count, BANDS * MOST, LEVELS)
    whitened = jnp.einsum(
        "arqsl,ns->arqnl", moved, select_low, preferred_element_type=jnp.float32
    )
    return (whitened.astype(jnp.bfloat16), inverse_root)


def solution(mesh):
    in_specs = (P("mem", "lat", None, None), P(), P())
    out_specs = (P("mem", None, "lat", None, None), P())
    return jax.shard_map(body, mesh=mesh, in_specs=in_specs, out_specs=out_specs, check_vma=False)
```

```python
import functools

import jax
import jax.numpy as jnp
import numpy as np
from jax import lax
from jax.experimental import pallas as pl
from jax.experimental.pallas import tpu as pltpu
from jax.sharding import PartitionSpec as P

NLAT = 160
NLON = 320
MM = 160
LEVELS = 128
BANDS = 16
MOST = 20
NS_ITERS = 6
CHIP_SIDE = 4

shrink_weight = 0.2


def legendre_kernel(lat_count, zonal_ref, start_ref, cosine_ref, weight_ref, out_ref, rows_ref):
    zonal = zonal_ref[...]
    zonal_square = zonal * zonal
    lanes = start_ref.shape[1] // 128
    start = [start_ref[:, 128 * c : 128 * (c + 1)] for c in range(lanes)]
    cosine = [cosine_ref[:, 128 * c : 128 * (c + 1)] for c in range(lanes)]
    weight = [weight_ref[:, 128 * c : 128 * (c + 1)] for c in range(lanes)]

    def advance(step, carry):
        for inner in range(8):
            index = step * 8 + inner
            degree = index.astype(jnp.float32)
            is_above = degree > zonal
            is_equal = degree == zonal
            upper_coef = jnp.sqrt(
                jnp.maximum(4.0 * degree * degree - 1.0, 1.0)
                / jnp.where(is_above, degree * degree - zonal_square, 1.0)
            )
            lower = degree - 1.0
            lower_coef = jnp.sqrt(
                jnp.maximum(lower * lower - zonal_square, 0.0)
                / jnp.maximum(4.0 * lower * lower - 1.0, 1.0)
            )
            following = []
            for c in range(lanes):
                previous, earlier = carry[2 * c], carry[2 * c + 1]
                climbed = upper_coef * (cosine[c] * previous - lower_coef * earlier)
                current = jnp.where(is_above, climbed, jnp.where(is_equal, start[c], 0.0))
                rows_ref[index, :, 128 * c : 128 * (c + 1)] = current * weight[c]
                following += [current, previous]
            carry = tuple(following)
        return carry

    zero = jnp.zeros_like(zonal)
    lax.fori_loop(0, MM // 8, advance, (zero,) * (2 * lanes))
    for q in range(out_ref.shape[0]):
        out_ref[q] = rows_ref[:, q, :][:, :lat_count].astype(jnp.bfloat16)


def legendre_table(zonal_orders, lat_count):
    owned = zonal_orders.shape[0]
    rows, lanes = 8, (lat_count + 127) // 128 * 128
    colatitude = np.pi * (np.arange(lat_count) + 0.5) / lat_count
    counter = np.arange(1, MM + 1)
    log_ratio = np.log((2.0 * counter - 1.0) / (2.0 * counter)).astype(np.float32)
    log_sine = np.log(np.sin(colatitude)).astype(np.float32)

    def spread(row):
        return np.tile(np.pad(row, (0, lanes - lat_count)).astype(np.float32), (rows, 1))

    cosine = spread(np.cos(colatitude))
    weight = spread(np.sqrt(np.pi / lat_count) * np.sin(colatitude))
    log_factor = jnp.sum(
        jnp.where(counter[None, :] <= zonal_orders[:, None], log_ratio[None, :], 0.0), axis=1
    )
    log_norm = 0.5 * jnp.log((2.0 * zonal_orders + 1.0) / 2.0) + 0.5 * log_factor
    start = jnp.exp(log_norm[:, None] + zonal_orders[:, None] * log_sine[None, :])
    start = jnp.pad(start, ((0, rows - owned), (0, lanes - lat_count)))
    zonal = jnp.broadcast_to(jnp.pad(zonal_orders, (0, rows - owned))[:, None], (rows, 128))
    return pl.pallas_call(
        functools.partial(legendre_kernel, lat_count),
        out_shape=jax.ShapeDtypeStruct((owned, MM, lat_count), jnp.bfloat16),
        in_specs=[pl.BlockSpec(memory_space=pltpu.VMEM)] * 4,
        out_specs=pl.BlockSpec(memory_space=pltpu.VMEM),
        scratch_shapes=[pltpu.VMEM((MM, rows, lanes), jnp.float32)],
        cost_estimate=pl.CostEstimate(
            flops=40_000_000, bytes_accessed=20_000_000, transcendentals=1_000_000
        ),
    )(zonal, start, cosine, weight)


def fourier_table(orders, lon_count):
    phases = np.arange(MM)[:, None] * np.arange(lon_count)[None, :] % lon_count
    angles = phases * (2.0 * np.pi / lon_count)
    scaling = np.sqrt(2.0 / lon_count)
    waves = np.stack([scaling * np.cos(angles), -scaling * np.sin(angles)])
    waves = jnp.asarray(waves.astype(np.float32)).astype(jnp.bfloat16)
    pick = (orders[:, None] == jnp.arange(MM, dtype=jnp.int32)[None, :]).astype(jnp.bfloat16)
    return jnp.einsum(
        "pm,rmk->rpk", pick, waves, preferred_element_type=jnp.float32
    ).astype(jnp.bfloat16)


def band_rows(band_widths):
    band_end = jnp.cumsum(band_widths)
    band_start = band_end - band_widths
    lowest = jnp.minimum(band_start, MM - MOST)
    slot_rows = lowest[:, None] + jnp.arange(MOST, dtype=jnp.int32)[None, :]
    band_keep = (slot_rows >= band_start[:, None]) & (slot_rows < band_end[:, None])
    return (band_start, band_end, slot_rows, band_keep)


def inverse_root_of(gram, denominator):
    row = lax.broadcasted_iota(jnp.int32, (LEVELS, LEVELS), 0)
    column = lax.broadcasted_iota(jnp.int32, (LEVELS, LEVELS), 1)
    identity = (row == column).astype(jnp.float32)

    def whole_sum(array):
        return jnp.sum(jnp.sum(array, axis=0, keepdims=True), axis=1, keepdims=True)

    def product(left, right):
        return lax.dot(
            left, right, precision=lax.Precision.HIGHEST, preferred_element_type=jnp.float32
        )

    covariance = gram / denominator
    spread = whole_sum(covariance * identity) / LEVELS
    shrunk = (1.0 - shrink_weight) * covariance + shrink_weight * spread * identity
    frobenius = jnp.sqrt(whole_sum(shrunk * shrunk) + 1e-06)
    growing = shrunk / frobenius
    inverse = 1.5 * identity - 0.5 * growing
    growing = product(growing, inverse)
    for iteration in range(NS_ITERS - 1):
        middle = 1.5 * identity - 0.5 * product(inverse, growing)
        if iteration < NS_ITERS - 2:
            growing = product(growing, middle)
        inverse = product(middle, inverse)
    return inverse / jnp.sqrt(frobenius)


def band_kernel(
    side,
    chips,
    members,
    gram_ref,
    denominator_ref,
    out_ref,
    pair,
    summed,
    got,
    own_ref,
    thin_got,
    full,
    pair_send,
    pair_recv,
    lat_send,
    lat_recv,
    thin_send,
    thin_recv,
    wide_send,
    wide_recv,
    half_send,
    half_recv,
    root_send,
    root_recv,
    pass_send,
    pass_recv,
):
    lat = lax.axis_index("lat")
    z = lax.axis_index("mem")
    core = lax.rem(lat, 2)
    chip = lax.div(lat, 2)
    partner = chip * 2 + 1 - core
    half = LEVELS // 2
    rows = pl.ds(pl.multiple_of(core * half, half), half)
    other_rows = pl.ds(pl.multiple_of((1 - core) * half, half), half)
    wide = chips // side

    def chip_after(d):
        x = lax.rem(lax.div(chip, side) + lax.div(d, side), wide)
        y = lax.rem(lax.rem(chip, side) + lax.rem(d, side), side)
        return x * side + y

    def chip_before(d):
        x = lax.rem(lax.div(chip, side) + wide - lax.div(d, side), wide)
        y = lax.rem(lax.rem(chip, side) + side - lax.rem(d, side), side)
        return x * side + y

    def z_after(d):
        return lax.rem(z + d, members)

    def tile_of(member):
        return pl.multiple_of(lax.div(member, 2) * 8, 8)

    def send(source, target, send_sem, recv_sem, device):
        return pltpu.make_async_remote_copy(
            src_ref=source,
            dst_ref=target,
            send_sem=send_sem,
            recv_sem=recv_sem,
            device_id=device,
            device_id_type=pl.DeviceIdType.MESH,
        )

    def each(first, last, work):
        def step(d, carry):
            work(d)
            return carry

        lax.fori_loop(first, last, step, 0)

    barrier = pltpu.get_barrier_semaphore()

    def greet(device):
        pl.semaphore_signal(
            barrier, inc=1, device_id=device, device_id_type=pl.DeviceIdType.MESH
        )

    each(1, members, lambda d: greet({"mem": z_after(d)}))
    each(1, chips, lambda d: greet({"lat": chip_after(d) * 2 + core}))
    greet({"lat": partner})
    pl.semaphore_wait(barrier, members + chips - 1)

    def pair_copy(d):
        return send(
            gram_ref.at[chip_after(d), other_rows],
            pair.at[d],
            pair_send.at[d],
            pair_recv.at[d],
            {"lat": partner},
        )

    def lat_copy(d):
        return send(
            summed.at[d],
            got.at[d],
            lat_send.at[d],
            lat_recv.at[d],
            {"lat": chip_after(d) * 2 + core},
        )

    each(1, chips, lambda d: pair_copy(d).start())
    pair_copy(0).start()

    def forward(d):
        pair_copy(d).wait_recv()
        summed[d] = gram_ref[chip_after(d), rows, :] + pair[d]
        lat_copy(d).start()

    each(1, chips, forward)
    pair_copy(0).wait_recv()
    own = gram_ref[chip, rows, :] + pair[0]

    def collect(d, total):
        lat_copy(d).wait_recv()
        return total + got[d]

    own_ref[...] = lax.fori_loop(1, chips, collect, own)

    def thin_copy(d):
        return send(
            own_ref.at[pl.ds(tile_of(z_after(d)), 8)],
            thin_got.at[d],
            thin_send.at[d],
            thin_recv.at[d],
            {"mem": z_after(d)},
        )

    each(1, members, lambda d: thin_copy(d).start())

    def thin_collect(d, total):
        thin_copy(d).wait_recv()
        return total + thin_got[d]

    tile = lax.fori_loop(1, members, thin_collect, own_ref[pl.ds(tile_of(z), 8), :])

    def tile_rows(member):
        return pl.ds(pl.multiple_of(core * half + tile_of(member), 8), 8)

    full[tile_rows(z), :] = tile

    def wide_copy(e, member):
        return send(
            full.at[tile_rows(member)],
            full.at[tile_rows(member)],
            wide_send.at[e],
            wide_recv.at[e],
            {"mem": z_after(2 * e)},
        )

    each(1, members // 2, lambda e: wide_copy(e, z).start())
    each(
        1, members // 2, lambda e: wide_copy(e, lax.rem(z + members - 2 * e, members)).wait_recv()
    )
    half_copy = send(
        full.at[rows], full.at[rows], half_send.at[0], half_recv.at[0], {"lat": partner}
    )
    half_arrival = send(
        full.at[other_rows], full.at[other_rows], half_send.at[0], half_recv.at[0], {"lat": partner}
    )
    half_copy.start()
    half_arrival.wait_recv()

    out_ref[chip] = inverse_root_of(full[...], denominator_ref[...])

    def root_copy(d, owner):
        return send(
            out_ref.at[owner, rows],
            out_ref.at[owner, rows],
            root_send.at[d],
            root_recv.at[d],
            {"lat": chip_after(d) * 2 + core},
        )

    def pass_copy(d, which):
        return send(
            out_ref.at[chip_before(d), which],
            out_ref.at[chip_before(d), which],
            pass_send.at[d],
            pass_recv.at[d],
            {"lat": partner},
        )

    each(1, chips, lambda d: root_copy(d, chip).start())

    def hand_over(d):
        root_copy(d, chip_before(d)).wait_recv()
        pass_copy(d, rows).start()

    each(1, chips, hand_over)

    def finish(d):
        pass_copy(d, other_rows).wait_recv()
        pass_copy(d, rows).wait_send()
        root_copy(d, chip).wait_send()
        lat_copy(d).wait_send()

    each(1, chips, finish)
    each(0, chips, lambda d: pair_copy(d).wait_send())
    each(1, members, lambda d: thin_copy(d).wait_send())
    each(1, members // 2, lambda e: wide_copy(e, z).wait_send())
    half_copy.wait_send()


def all_inverse_roots(partial_gram, denominator, side):
    chips = partial_gram.shape[0]
    members = lax.axis_size("mem")
    half = LEVELS // 2
    dma = pltpu.SemaphoreType.DMA
    return pl.pallas_call(
        functools.partial(band_kernel, side, chips, members),
        out_shape=jax.ShapeDtypeStruct((chips, LEVELS, LEVELS), jnp.float32),
        in_specs=[pl.BlockSpec(memory_space=pltpu.VMEM)] * 2,
        out_specs=pl.BlockSpec(memory_space=pltpu.VMEM),
        scratch_shapes=[
            pltpu.VMEM((chips, half, LEVELS), jnp.float32),
            pltpu.VMEM((chips, half, LEVELS), jnp.float32),
            pltpu.VMEM((chips, half, LEVELS), jnp.float32),
            pltpu.VMEM((half, LEVELS), jnp.float32),
            pltpu.VMEM((members, 8, LEVELS), jnp.float32),
            pltpu.VMEM((LEVELS, LEVELS), jnp.float32),
            dma((chips,)),
            dma((chips,)),
            dma((chips,)),
            dma((chips,)),
            dma((members,)),
            dma((members,)),
            dma((members // 2,)),
            dma((members // 2,)),
            dma((1,)),
            dma((1,)),
            dma((chips,)),
            dma((chips,)),
            dma((chips,)),
            dma((chips,)),
        ],
        compiler_params=pltpu.CompilerParams(collective_id=0, has_side_effects=True),
    )(partial_gram, denominator)


def body(perturbation, owner_map, band_widths):
    members = perturbation.shape[0]
    lat_rows = perturbation.shape[1]
    lat_devices = lax.axis_size("lat")
    lat_index = lax.axis_index("lat")
    owned_count = MM // lat_devices
    wave_table = fourier_table(owner_map, NLON)
    waves = jnp.einsum(
        "rpk,ajkl->arpjl", wave_table, perturbation, preferred_element_type=jnp.float32
    ).astype(jnp.bfloat16)
    owned_waves = lax.dynamic_slice_in_dim(owner_map, lat_index * owned_count, owned_count, 0)
    poly_table = legendre_table(owned_waves.astype(jnp.float32), lat_rows * lat_devices)
    spectral = jnp.einsum(
        "qnj,arqjl->arqnl",
        poly_table,
        lax.all_to_all(waves, "lat", split_axis=2, concat_axis=3, tiled=True),
        preferred_element_type=jnp.float32,
    ).astype(jnp.bfloat16)
    band_start, band_end, slot_rows, band_keep = band_rows(band_widths)
    row_index = jnp.arange(MM, dtype=jnp.int32)
    selector = (row_index[:, None] == slot_rows.reshape(-1)[None, :]) & band_keep.reshape(-1)[
        None, :
    ]
    select_low = selector.astype(jnp.bfloat16)
    masked = jnp.einsum(
        "arqnl,ns->arqsl", spectral, select_low, preferred_element_type=jnp.float32
    ).astype(jnp.bfloat16)
    masked = masked.reshape(members, 2, owned_count, BANDS, MOST, LEVELS)
    partial_gram = jnp.einsum(
        "arqbtk,arqbtl->bkl", masked, masked, preferred_element_type=jnp.float32
    )
    member_total = members * lax.axis_size("mem")
    bands_here = lax.axis_size("lat") // BANDS
    band = lat_index // bands_here
    own_start = lax.dynamic_slice_in_dim(band_start, band, 1, 0)
    own_end = lax.dynamic_slice_in_dim(band_end, band, 1, 0)
    span = (own_end * own_end - own_start * own_start).astype(jnp.float32)
    denominator = jnp.broadcast_to((member_total - 1.0) * span[:, None], (1, LEVELS))
    inverse_root = all_inverse_roots(partial_gram, denominator, CHIP_SIDE)
    root_low = inverse_root.astype(jnp.bfloat16)
    moved = jnp.einsum("arqbtk,blk->arqbtl", masked, root_low, preferred_element_type=jnp.float32)
    moved = moved.astype(jnp.bfloat16).reshape(members, 2, owned_count, BANDS * MOST, LEVELS)
    whitened = jnp.einsum(
        "arqsl,ns->arqnl", moved, select_low, preferred_element_type=jnp.float32
    )
    return (whitened.astype(jnp.bfloat16), inverse_root)


def solution(mesh):
    in_specs = (P("mem", "lat", None, None), P(), P())
    out_specs = (P("mem", None, "lat", None, None), P())
    return jax.shard_map(body, mesh=mesh, in_specs=in_specs, out_specs=out_specs, check_vma=False)
```

```python
import functools

import jax
import jax.numpy as jnp
import numpy as np
from jax import lax
from jax.experimental import pallas as pl
from jax.experimental.pallas import tpu as pltpu
from jax.sharding import PartitionSpec as P

NLAT = 160
NLON = 320
MM = 160
LEVELS = 128
BANDS = 16
NS_ITERS = 6
CHIP_SIDE = 4
SLOTS = 32

shrink_weight = 0.2


def legendre_rows(zonal_ref, start_ref, cosine_ref, weight_ref, rows_ref):
    zonal = zonal_ref[...]
    zonal_square = zonal * zonal
    lanes = start_ref.shape[1] // 128
    start = [start_ref[:, 128 * c : 128 * (c + 1)] for c in range(lanes)]
    cosine = [cosine_ref[:, 128 * c : 128 * (c + 1)] for c in range(lanes)]
    weight = [weight_ref[:, 128 * c : 128 * (c + 1)] for c in range(lanes)]

    def advance(step, carry):
        for inner in range(8):
            index = step * 8 + inner
            degree = index.astype(jnp.float32)
            is_above = degree > zonal
            is_equal = degree == zonal
            upper_coef = jnp.sqrt(
                jnp.maximum(4.0 * degree * degree - 1.0, 1.0)
                / jnp.where(is_above, degree * degree - zonal_square, 1.0)
            )
            lower = degree - 1.0
            lower_coef = jnp.sqrt(
                jnp.maximum(lower * lower - zonal_square, 0.0)
                / jnp.maximum(4.0 * lower * lower - 1.0, 1.0)
            )
            following = []
            for c in range(lanes):
                previous, earlier = carry[2 * c], carry[2 * c + 1]
                climbed = upper_coef * (cosine[c] * previous - lower_coef * earlier)
                current = jnp.where(is_above, climbed, jnp.where(is_equal, start[c], 0.0))
                rows_ref[index, :, 128 * c : 128 * (c + 1)] = current * weight[c]
                following += [current, previous]
            carry = tuple(following)
        return carry

    zero = jnp.zeros_like(zonal)
    lax.fori_loop(0, MM // 8, advance, (zero,) * (2 * lanes))


def legendre_start(zonal_orders, lat_count, lat_rows):
    owned = zonal_orders.shape[0]
    rows, lanes = 8, (lat_count + 127) // 128 * 128
    devices = lat_count // lat_rows
    place = np.arange(lat_count)
    colatitude = np.pi * (place % devices * lat_rows + place // devices + 0.5) / lat_count
    counter = np.arange(1, MM + 1)
    log_ratio = np.log((2.0 * counter - 1.0) / (2.0 * counter)).astype(np.float32)
    log_sine = np.log(np.sin(colatitude)).astype(np.float32)

    def spread(row):
        return np.tile(np.pad(row, (0, lanes - lat_count)).astype(np.float32), (rows, 1))

    cosine = spread(np.cos(colatitude))
    weight = spread(np.sqrt(np.pi / lat_count) * np.sin(colatitude))
    log_factor = jnp.sum(
        jnp.where(counter[None, :] <= zonal_orders[:, None], log_ratio[None, :], 0.0), axis=1
    )
    log_norm = 0.5 * jnp.log((2.0 * zonal_orders + 1.0) / 2.0) + 0.5 * log_factor
    start = jnp.exp(log_norm[:, None] + zonal_orders[:, None] * log_sine[None, :])
    start = jnp.pad(start, ((0, rows - owned), (0, lanes - lat_count)))
    zonal = jnp.broadcast_to(jnp.pad(zonal_orders, (0, rows - owned))[:, None], (rows, 128))
    return (zonal, start, cosine, weight)


def fourier_table(orders, lon_count):
    phases = np.arange(MM)[:, None] * np.arange(lon_count)[None, :] % lon_count
    angles = phases * (2.0 * np.pi / lon_count)
    scaling = np.sqrt(2.0 / lon_count)
    waves = np.stack([scaling * np.cos(angles), -scaling * np.sin(angles)])
    waves = jnp.asarray(waves.astype(np.float32)).astype(jnp.bfloat16)
    pick = (orders[:, None] == jnp.arange(MM, dtype=jnp.int32)[None, :]).astype(jnp.bfloat16)
    return jnp.einsum(
        "pm,rmk->rpk", pick, waves, preferred_element_type=jnp.float32
    ).astype(jnp.bfloat16)


def inverse_root_of(gram, denominator):
    row = lax.broadcasted_iota(jnp.int32, (LEVELS, LEVELS), 0)
    column = lax.broadcasted_iota(jnp.int32, (LEVELS, LEVELS), 1)
    identity = (row == column).astype(jnp.float32)

    def whole_sum(array):
        return jnp.sum(jnp.sum(array, axis=0, keepdims=True), axis=1, keepdims=True)

    def product(left, right):
        return lax.dot(
            left, right, precision=lax.Precision.HIGHEST, preferred_element_type=jnp.float32
        )

    covariance = gram / denominator
    spread = whole_sum(covariance * identity) / LEVELS
    shrunk = (1.0 - shrink_weight) * covariance + shrink_weight * spread * identity
    frobenius = jnp.sqrt(whole_sum(shrunk * shrunk) + 1e-06)
    growing = shrunk / frobenius
    inverse = 1.5 * identity - 0.5 * growing
    growing = product(growing, inverse)
    for iteration in range(NS_ITERS - 1):
        middle = 1.5 * identity - 0.5 * product(inverse, growing)
        if iteration < NS_ITERS - 2:
            growing = product(growing, middle)
        inverse = product(middle, inverse)
    return inverse / jnp.sqrt(frobenius)


def band_kernel(
    side,
    chips,
    members,
    waves_ref,
    zonal_ref,
    start_ref,
    cosine_ref,
    weight_ref,
    select_ref,
    spread_ref,
    denominator_ref,
    white_ref,
    out_ref,
    rows_ref,
    arrived,
    grid,
    masked,
    moved,
    gram_ref,
    pair,
    summed,
    got,
    own_ref,
    thin_got,
    full,
    wave_send,
    wave_recv,
    pair_send,
    pair_recv,
    lat_send,
    lat_recv,
    thin_send,
    thin_recv,
    wide_send,
    wide_recv,
    half_send,
    half_recv,
    root_send,
    root_recv,
    pass_send,
    pass_recv,
):
    lat = lax.axis_index("lat")
    z = lax.axis_index("mem")
    core = lax.rem(lat, 2)
    chip = lax.div(lat, 2)
    partner = chip * 2 + 1 - core
    half = LEVELS // 2
    rows = pl.ds(pl.multiple_of(core * half, half), half)
    other_rows = pl.ds(pl.multiple_of((1 - core) * half, half), half)
    wide = chips // side

    def chip_after(d):
        x = lax.rem(lax.div(chip, side) + lax.div(d, side), wide)
        y = lax.rem(lax.rem(chip, side) + lax.rem(d, side), side)
        return x * side + y

    def chip_before(d):
        x = lax.rem(lax.div(chip, side) + wide - lax.div(d, side), wide)
        y = lax.rem(lax.rem(chip, side) + side - lax.rem(d, side), side)
        return x * side + y

    def lat_after(d):
        return chip_after(lax.div(d, 2)) * 2 + lax.rem(core + lax.rem(d, 2), 2)

    def lat_before(d):
        return chip_before(lax.div(d, 2)) * 2 + lax.rem(core + lax.rem(d, 2), 2)

    def z_after(d):
        return lax.rem(z + d, members)

    def tile_of(member):
        return pl.multiple_of(lax.div(member, 2) * 8, 8)

    def send(source, target, send_sem, recv_sem, device):
        return pltpu.make_async_remote_copy(
            src_ref=source,
            dst_ref=target,
            send_sem=send_sem,
            recv_sem=recv_sem,
            device_id=device,
            device_id_type=pl.DeviceIdType.MESH,
        )

    def each(first, last, work):
        def step(d, carry):
            work(d)
            return carry

        lax.fori_loop(first, last, step, 0)

    barrier = pltpu.get_barrier_semaphore()

    def greet(device):
        pl.semaphore_signal(
            barrier, inc=1, device_id=device, device_id_type=pl.DeviceIdType.MESH
        )

    each(1, members, lambda d: greet({"mem": z_after(d)}))
    each(1, 2 * chips, lambda d: greet({"lat": lat_after(d)}))
    legendre_rows(zonal_ref, start_ref, cosine_ref, weight_ref, rows_ref)
    pl.semaphore_wait(barrier, members - 1 + 2 * chips - 1)

    def wave_copy(d, source):
        return send(
            waves_ref.at[lat_after(d)],
            arrived.at[source],
            wave_send.at[d],
            wave_recv.at[d],
            {"lat": lat_after(d)},
        )

    each(1, 2 * chips, lambda d: wave_copy(d, lat).start())
    arrived[lat] = waves_ref[lat]
    each(1, 2 * chips, lambda d: wave_copy(d, lat_before(d)).wait_recv())
    devices, per_device = arrived.shape[0], arrived.shape[1]
    owned = masked.shape[0]
    lat_rows = per_device // (2 * owned)
    stride = grid.shape[0] // (devices + 1)
    for device in range(devices):
        grid[device * stride : device * stride + per_device] = arrived[device].astype(jnp.float32)

    def field(r, q):
        first = (r * owned + q) * lat_rows
        parts = [grid[pl.ds(first + k, devices, stride=stride), :] for k in range(lat_rows)]
        return jnp.concatenate(parts, axis=0)

    for q in range(owned):
        table = rows_ref[:, q, :][:, : devices * lat_rows].astype(jnp.bfloat16)
        both = jnp.concatenate([field(0, q), field(1, q)], axis=1).astype(jnp.bfloat16)
        coefficients = jnp.dot(table, both, preferred_element_type=jnp.float32)
        masked[q] = jnp.dot(
            select_ref[...],
            coefficients.astype(jnp.bfloat16),
            preferred_element_type=jnp.float32,
        ).astype(jnp.bfloat16)

    def band_slots(band):
        return pl.ds(pl.multiple_of(band * SLOTS, SLOTS), SLOTS)

    def band_values(band):
        slots = band_slots(band)
        return jnp.concatenate(
            [
                masked[q, slots, LEVELS * r : LEVELS * (r + 1)]
                for q in range(owned)
                for r in range(2)
            ],
            axis=0,
        )

    def add_up(band):
        values = band_values(band)
        gram_ref[band] = lax.dot_general(
            values, values, (((0,), (0,)), ((), ())), preferred_element_type=jnp.float32
        )

    def whiten(band):
        root_low = out_ref[band].astype(jnp.bfloat16)
        turned = lax.dot_general(
            band_values(band),
            root_low,
            (((1,), (1,)), ((), ())),
            preferred_element_type=jnp.float32,
        ).astype(jnp.bfloat16)
        slots = band_slots(band)
        for q in range(owned):
            for r in range(2):
                row = (2 * q + r) * SLOTS
                moved[q, slots, LEVELS * r : LEVELS * (r + 1)] = turned[row : row + SLOTS]

    def pair_copy(d):
        return send(
            gram_ref.at[chip_after(d), other_rows],
            pair.at[d],
            pair_send.at[d],
            pair_recv.at[d],
            {"lat": partner},
        )

    def lat_copy(d):
        return send(
            summed.at[d],
            got.at[d],
            lat_send.at[d],
            lat_recv.at[d],
            {"lat": chip_after(d) * 2 + core},
        )

    def begin(d):
        add_up(chip_after(d))
        pair_copy(d).start()

    each(1, chips, begin)
    begin(0)

    def forward(d):
        pair_copy(d).wait_recv()
        summed[d] = gram_ref[chip_after(d), rows, :] + pair[d]
        lat_copy(d).start()

    each(1, chips, forward)
    pair_copy(0).wait_recv()
    own = gram_ref[chip, rows, :] + pair[0]

    def collect(d, total):
        lat_copy(d).wait_recv()
        return total + got[d]

    own_ref[...] = lax.fori_loop(1, chips, collect, own)

    def thin_copy(d):
        return send(
            own_ref.at[pl.ds(tile_of(z_after(d)), 8)],
            thin_got.at[d],
            thin_send.at[d],
            thin_recv.at[d],
            {"mem": z_after(d)},
        )

    each(1, members, lambda d: thin_copy(d).start())

    def thin_collect(d, total):
        thin_copy(d).wait_recv()
        return total + thin_got[d]

    tile = lax.fori_loop(1, members, thin_collect, own_ref[pl.ds(tile_of(z), 8), :])

    def tile_rows(member):
        return pl.ds(pl.multiple_of(core * half + tile_of(member), 8), 8)

    full[tile_rows(z), :] = tile

    def wide_copy(e, member):
        return send(
            full.at[tile_rows(member)],
            full.at[tile_rows(member)],
            wide_send.at[e],
            wide_recv.at[e],
            {"mem": z_after(2 * e)},
        )

    each(1, members // 2, lambda e: wide_copy(e, z).start())
    each(
        1, members // 2, lambda e: wide_copy(e, lax.rem(z + members - 2 * e, members)).wait_recv()
    )
    half_copy = send(
        full.at[rows], full.at[rows], half_send.at[0], half_recv.at[0], {"lat": partner}
    )
    half_arrival = send(
        full.at[other_rows], full.at[other_rows], half_send.at[0], half_recv.at[0], {"lat": partner}
    )
    half_copy.start()
    half_arrival.wait_recv()

    out_ref[chip] = inverse_root_of(full[...], denominator_ref[...])

    def root_copy(d, owner):
        return send(
            out_ref.at[owner, rows],
            out_ref.at[owner, rows],
            root_send.at[d],
            root_recv.at[d],
            {"lat": chip_after(d) * 2 + core},
        )

    def pass_copy(d, which):
        return send(
            out_ref.at[chip_before(d), which],
            out_ref.at[chip_before(d), which],
            pass_send.at[d],
            pass_recv.at[d],
            {"lat": partner},
        )

    each(1, chips, lambda d: root_copy(d, chip).start())

    whiten(chip)

    def hand_over(d):
        root_copy(d, chip_before(d)).wait_recv()
        pass_copy(d, rows).start()

    def take_over(d):
        pass_copy(d, other_rows).wait_recv()
        whiten(chip_before(d))

    def both_ways(d):
        hand_over(d)
        take_over(d - 1)

    hand_over(1)
    each(2, chips, both_ways)
    take_over(chips - 1)
    for q in range(owned):
        result = jnp.dot(
            spread_ref[...], moved[q], preferred_element_type=jnp.float32
        ).astype(jnp.bfloat16)
        for r in range(2):
            white_ref[r, q] = result[:, LEVELS * r : LEVELS * (r + 1)]

    def finish(d):
        pass_copy(d, rows).wait_send()
        root_copy(d, chip).wait_send()
        lat_copy(d).wait_send()

    each(1, chips, finish)
    each(0, chips, lambda d: pair_copy(d).wait_send())
    each(1, 2 * chips, lambda d: wave_copy(d, lat).wait_send())
    each(1, members, lambda d: thin_copy(d).wait_send())
    each(1, members // 2, lambda e: wide_copy(e, z).wait_send())
    half_copy.wait_send()


def transformed(waves, table_parts, select, denominator, owned, side):
    devices, per_device = waves.shape[:2]
    chips = devices // 2
    members = lax.axis_size("mem")
    half = LEVELS // 2
    dma = pltpu.SemaphoreType.DMA
    stride = (per_device + 7) // 8 * 8
    counts = [devices, chips, chips, members, members // 2, 1, chips, chips]
    return pl.pallas_call(
        functools.partial(band_kernel, side, chips, members),
        out_shape=(
            jax.ShapeDtypeStruct((2, owned, MM, LEVELS), jnp.bfloat16),
            jax.ShapeDtypeStruct((chips, LEVELS, LEVELS), jnp.float32),
        ),
        in_specs=[pl.BlockSpec(memory_space=pltpu.VMEM)] * 8,
        out_specs=(pl.BlockSpec(memory_space=pltpu.VMEM),) * 2,
        scratch_shapes=[
            pltpu.VMEM((MM, *table_parts[1].shape), jnp.float32),
            pltpu.VMEM(waves.shape, jnp.bfloat16),
            pltpu.VMEM(((devices + 1) * stride, LEVELS), jnp.float32),
            pltpu.VMEM((owned, chips * SLOTS, 2 * LEVELS), jnp.bfloat16),
            pltpu.VMEM((owned, chips * SLOTS, 2 * LEVELS), jnp.bfloat16),
            pltpu.VMEM((chips, LEVELS, LEVELS), jnp.float32),
            pltpu.VMEM((chips, half, LEVELS), jnp.float32),
            pltpu.VMEM((chips, half, LEVELS), jnp.float32),
            pltpu.VMEM((chips, half, LEVELS), jnp.float32),
            pltpu.VMEM((half, LEVELS), jnp.float32),
            pltpu.VMEM((members, 8, LEVELS), jnp.float32),
            pltpu.VMEM((LEVELS, LEVELS), jnp.float32),
        ]
        + [dma((count,)) for count in counts for way in range(2)],
        compiler_params=pltpu.CompilerParams(
            collective_id=0, has_side_effects=True, vmem_limit_bytes=48 * 2**20
        ),
    )(waves, *table_parts, select, select.T, denominator)


def body(perturbation, owner_map, band_widths):
    members, lat_rows = perturbation.shape[:2]
    lat_devices = lax.axis_size("lat")
    lat_index = lax.axis_index("lat")
    owned = MM // lat_devices
    wave_table = fourier_table(owner_map, NLON).reshape(2, lat_devices, owned, NLON)
    waves = jnp.einsum(
        "rdqk,jkl->drqjl", wave_table, perturbation[0], preferred_element_type=jnp.float32
    ).astype(jnp.bfloat16)
    waves = waves.reshape(lat_devices, 2 * owned * lat_rows, LEVELS)
    owned_waves = lax.dynamic_slice_in_dim(owner_map, lat_index * owned, owned, 0)
    table_parts = legendre_start(
        owned_waves.astype(jnp.float32), lat_rows * lat_devices, lat_rows
    )
    band_end = jnp.cumsum(band_widths)
    band_start = band_end - band_widths
    slot = jnp.arange(SLOTS, dtype=jnp.int32)[None, :]
    slot_row = jnp.where(slot < band_widths[:, None], band_start[:, None] + slot, -1)
    row_index = jnp.arange(MM, dtype=jnp.int32)
    select = (slot_row.reshape(-1)[:, None] == row_index[None, :]).astype(jnp.bfloat16)
    member_total = members * lax.axis_size("mem")
    band = lat_index // (lat_devices // BANDS)
    own_start = lax.dynamic_slice_in_dim(band_start, band, 1, 0)
    own_end = lax.dynamic_slice_in_dim(band_end, band, 1, 0)
    span = (own_end * own_end - own_start * own_start).astype(jnp.float32)
    denominator = jnp.broadcast_to((member_total - 1.0) * span[:, None], (1, LEVELS))
    whitened, inverse_root = transformed(
        waves, table_parts, select, denominator, owned, CHIP_SIDE
    )
    return (whitened[None], inverse_root)


def solution(mesh):
    in_specs = (P("mem", "lat", None, None), P(), P())
    out_specs = (P("mem", None, "lat", None, None), P())
    return jax.shard_map(body, mesh=mesh, in_specs=in_specs, out_specs=out_specs, check_vma=False)
```

```python
import functools

import jax
import jax.numpy as jnp
import numpy as np
from jax import lax
from jax.experimental import pallas as pl
from jax.experimental.pallas import tpu as pltpu
from jax.sharding import PartitionSpec as P

NLAT = 160
NLON = 320
MM = 160
LEVELS = 128
BANDS = 16
NS_ITERS = 6
CHIP_SIDE = 4
SLOTS = 32

shrink_weight = 0.2


def legendre_rows(zonal, start_ref, cosine_ref, weight_ref, rows_ref):
    zonal_square = zonal * zonal
    lanes = start_ref.shape[1] // 128
    start = [start_ref[:, 128 * c : 128 * (c + 1)] for c in range(lanes)]
    cosine = [cosine_ref[:, 128 * c : 128 * (c + 1)] for c in range(lanes)]
    weight = [weight_ref[:, 128 * c : 128 * (c + 1)] for c in range(lanes)]

    def advance(step, carry):
        for inner in range(8):
            index = step * 8 + inner
            degree = index.astype(jnp.float32)
            is_above = degree > zonal
            is_equal = degree == zonal
            upper_coef = jnp.sqrt(
                jnp.maximum(4.0 * degree * degree - 1.0, 1.0)
                / jnp.where(is_above, degree * degree - zonal_square, 1.0)
            )
            lower = degree - 1.0
            lower_coef = jnp.sqrt(
                jnp.maximum(lower * lower - zonal_square, 0.0)
                / jnp.maximum(4.0 * lower * lower - 1.0, 1.0)
            )
            following = []
            for c in range(lanes):
                previous, earlier = carry[2 * c], carry[2 * c + 1]
                climbed = upper_coef * (cosine[c] * previous - lower_coef * earlier)
                current = jnp.where(is_above, climbed, jnp.where(is_equal, start[c], 0.0))
                rows_ref[index, :, 128 * c : 128 * (c + 1)] = current * weight[c]
                following += [current, previous]
            carry = tuple(following)
        return carry

    zero = jnp.zeros_like(zonal)
    lax.fori_loop(0, MM // 8, advance, (zero,) * (2 * lanes))


def latitude_rows(lat_count, lat_rows):
    rows, lanes = 8, (max(lat_count, MM) + 127) // 128 * 128
    devices = lat_count // lat_rows
    place = np.arange(lat_count)
    colatitude = np.pi * (place % devices * lat_rows + place // devices + 0.5) / lat_count
    counter = np.arange(1, MM + 1)
    log_ratio = np.log((2.0 * counter - 1.0) / (2.0 * counter))

    def spread(row):
        return np.tile(np.pad(row, (0, lanes - row.size)).astype(np.float32), (rows, 1))

    sine = np.sin(colatitude)
    weight = np.sqrt(np.pi / lat_count) * sine
    return (spread(log_ratio), spread(np.log(sine)), spread(np.cos(colatitude)), spread(weight))


def owned_orders(owner, first):
    rows, count = 8, owner.shape[1]
    row = lax.broadcasted_iota(jnp.int32, (rows, count), 0)
    place = lax.broadcasted_iota(jnp.int32, (rows, count), 1)
    held = jnp.broadcast_to(owner.astype(jnp.float32), (rows, count))
    return jnp.sum(jnp.where(place == first + row, held, 0.0), axis=1, keepdims=True)


def first_values(orders, log_ratio, log_sine):
    counter = lax.broadcasted_iota(jnp.int32, log_ratio.shape, 1).astype(jnp.float32) + 1.0
    log_factor = jnp.sum(jnp.where(counter <= orders, log_ratio, 0.0), axis=1, keepdims=True)
    log_norm = 0.5 * jnp.log((2.0 * orders + 1.0) / 2.0) + 0.5 * log_factor
    return jnp.exp(log_norm + orders * log_sine)


def slot_selectors(widths, bands, total):
    slots, lanes = bands * SLOTS, widths.shape[1]
    wide = widths.astype(jnp.float32)
    band = lax.broadcasted_iota(jnp.int32, (slots, lanes), 0) // SLOTS
    other = lax.broadcasted_iota(jnp.int32, (slots, lanes), 1)
    rows = jnp.broadcast_to(wide, (slots, lanes))
    start = jnp.sum(jnp.where(other < band, rows, 0.0), axis=1, keepdims=True)
    width = jnp.sum(jnp.where(other == band, rows, 0.0), axis=1, keepdims=True)
    place = (lax.broadcasted_iota(jnp.int32, (slots, 1), 0) % SLOTS).astype(jnp.float32)
    degree = jnp.where(place < width, start + place, -1.0)
    row = lax.broadcasted_iota(jnp.int32, (slots, total), 1).astype(jnp.float32)
    return jnp.where(degree == row, 1.0, 0.0)


def band_span(widths, band):
    other = lax.broadcasted_iota(jnp.int32, widths.shape, 1)
    wide = widths.astype(jnp.float32)
    start = jnp.sum(jnp.where(other < band, wide, 0.0), axis=1, keepdims=True)
    end = jnp.sum(jnp.where(other <= band, wide, 0.0), axis=1, keepdims=True)
    return end * end - start * start


def fourier_table(orders, lon_count):
    phases = np.arange(MM)[:, None] * np.arange(lon_count)[None, :] % lon_count
    angles = phases * (2.0 * np.pi / lon_count)
    scaling = np.sqrt(2.0 / lon_count)
    waves = np.stack([scaling * np.cos(angles), -scaling * np.sin(angles)])
    waves = jnp.asarray(waves.astype(np.float32)).astype(jnp.bfloat16)
    pick = (orders[:, None] == jnp.arange(MM, dtype=jnp.int32)[None, :]).astype(jnp.bfloat16)
    return jnp.einsum(
        "pm,rmk->rpk", pick, waves, preferred_element_type=jnp.float32
    ).astype(jnp.bfloat16)


def inverse_root_of(gram, denominator):
    row = lax.broadcasted_iota(jnp.int32, (LEVELS, LEVELS), 0)
    column = lax.broadcasted_iota(jnp.int32, (LEVELS, LEVELS), 1)
    identity = (row == column).astype(jnp.float32)

    def whole_sum(array):
        return jnp.sum(jnp.sum(array, axis=0, keepdims=True), axis=1, keepdims=True)

    def product(left, right):
        return lax.dot(
            left, right, precision=lax.Precision.HIGHEST, preferred_element_type=jnp.float32
        )

    covariance = gram / denominator
    spread = whole_sum(covariance * identity) / LEVELS
    shrunk = (1.0 - shrink_weight) * covariance + shrink_weight * spread * identity
    frobenius = jnp.sqrt(whole_sum(shrunk * shrunk) + 1e-06)
    growing = shrunk / frobenius
    inverse = 1.5 * identity - 0.5 * growing
    growing = product(growing, inverse)
    for iteration in range(NS_ITERS - 1):
        middle = 1.5 * identity - 0.5 * product(inverse, growing)
        if iteration < NS_ITERS - 2:
            growing = product(growing, middle)
        inverse = product(middle, inverse)
    return inverse / jnp.sqrt(frobenius)


def band_kernel(
    side,
    chips,
    members,
    waves_ref,
    owner_ref,
    widths_ref,
    ratio_ref,
    sine_ref,
    cosine_ref,
    weight_ref,
    white_ref,
    out_ref,
    rows_ref,
    start_ref,
    select_ref,
    spread_ref,
    arrived,
    grid,
    masked,
    moved,
    gram_ref,
    pair,
    summed,
    got,
    own_ref,
    thin_got,
    full,
    wave_send,
    wave_recv,
    pair_send,
    pair_recv,
    lat_send,
    lat_recv,
    thin_send,
    thin_recv,
    wide_send,
    wide_recv,
    half_send,
    half_recv,
    root_send,
    root_recv,
    pass_send,
    pass_recv,
):
    lat = lax.axis_index("lat")
    z = lax.axis_index("mem")
    core = lax.rem(lat, 2)
    chip = lax.div(lat, 2)
    partner = chip * 2 + 1 - core
    half = LEVELS // 2
    rows = pl.ds(pl.multiple_of(core * half, half), half)
    other_rows = pl.ds(pl.multiple_of((1 - core) * half, half), half)
    wide = chips // side

    def chip_after(d):
        x = lax.rem(lax.div(chip, side) + lax.div(d, side), wide)
        y = lax.rem(lax.rem(chip, side) + lax.rem(d, side), side)
        return x * side + y

    def chip_before(d):
        x = lax.rem(lax.div(chip, side) + wide - lax.div(d, side), wide)
        y = lax.rem(lax.rem(chip, side) + side - lax.rem(d, side), side)
        return x * side + y

    def lat_after(d):
        return chip_after(lax.div(d, 2)) * 2 + lax.rem(core + lax.rem(d, 2), 2)

    def lat_before(d):
        return chip_before(lax.div(d, 2)) * 2 + lax.rem(core + lax.rem(d, 2), 2)

    def z_after(d):
        return lax.rem(z + d, members)

    def tile_of(member):
        return pl.multiple_of(lax.div(member, 2) * 8, 8)

    def send(source, target, send_sem, recv_sem, device):
        return pltpu.make_async_remote_copy(
            src_ref=source,
            dst_ref=target,
            send_sem=send_sem,
            recv_sem=recv_sem,
            device_id=device,
            device_id_type=pl.DeviceIdType.MESH,
        )

    def each(first, last, work):
        def step(d, carry):
            work(d)
            return carry

        lax.fori_loop(first, last, step, 0)

    barrier = pltpu.get_barrier_semaphore()

    def greet(device):
        pl.semaphore_signal(
            barrier, inc=1, device_id=device, device_id_type=pl.DeviceIdType.MESH
        )

    each(1, members, lambda d: greet({"mem": z_after(d)}))
    each(1, 2 * chips, lambda d: greet({"lat": lat_after(d)}))
    orders = owned_orders(owner_ref[...], lat * masked.shape[0])
    start_ref[...] = first_values(orders, ratio_ref[...], sine_ref[...])
    zonal = jnp.broadcast_to(orders, (orders.shape[0], 128))
    select = slot_selectors(widths_ref[...], chips, select_ref.shape[1])
    select_ref[...] = select.astype(jnp.bfloat16)
    spread_ref[...] = jnp.transpose(select).astype(jnp.bfloat16)
    legendre_rows(zonal, start_ref, cosine_ref, weight_ref, rows_ref)
    pl.semaphore_wait(barrier, members - 1 + 2 * chips - 1)

    def wave_copy(d, source):
        return send(
            waves_ref.at[lat_after(d)],
            arrived.at[source],
            wave_send.at[d],
            wave_recv.at[d],
            {"lat": lat_after(d)},
        )

    each(1, 2 * chips, lambda d: wave_copy(d, lat).start())
    arrived[lat] = waves_ref[lat]
    each(1, 2 * chips, lambda d: wave_copy(d, lat_before(d)).wait_recv())
    devices, per_device = arrived.shape[0], arrived.shape[1]
    owned = masked.shape[0]
    lat_rows = per_device // (2 * owned)
    stride = grid.shape[0] // (devices + 1)
    for device in range(devices):
        grid[device * stride : device * stride + per_device] = arrived[device].astype(jnp.float32)

    def field(r, q):
        first = (r * owned + q) * lat_rows
        parts = [grid[pl.ds(first + k, devices, stride=stride), :] for k in range(lat_rows)]
        return jnp.concatenate(parts, axis=0)

    for q in range(owned):
        table = rows_ref[:, q, :][:, : devices * lat_rows].astype(jnp.bfloat16)
        both = jnp.concatenate([field(0, q), field(1, q)], axis=1).astype(jnp.bfloat16)
        coefficients = jnp.dot(table, both, preferred_element_type=jnp.float32)
        masked[q] = jnp.dot(
            select_ref[:, :MM],
            coefficients.astype(jnp.bfloat16),
            preferred_element_type=jnp.float32,
        ).astype(jnp.bfloat16)

    def band_slots(band):
        return pl.ds(pl.multiple_of(band * SLOTS, SLOTS), SLOTS)

    def band_values(band):
        slots = band_slots(band)
        return jnp.concatenate(
            [
                masked[q, slots, LEVELS * r : LEVELS * (r + 1)]
                for q in range(owned)
                for r in range(2)
            ],
            axis=0,
        )

    def add_up(band):
        values = band_values(band)
        gram_ref[band] = lax.dot_general(
            values, values, (((0,), (0,)), ((), ())), preferred_element_type=jnp.float32
        )

    def whiten(band):
        root_low = out_ref[band].astype(jnp.bfloat16)
        turned = lax.dot_general(
            band_values(band),
            root_low,
            (((1,), (1,)), ((), ())),
            preferred_element_type=jnp.float32,
        ).astype(jnp.bfloat16)
        slots = band_slots(band)
        for q in range(owned):
            for r in range(2):
                row = (2 * q + r) * SLOTS
                moved[q, slots, LEVELS * r : LEVELS * (r + 1)] = turned[row : row + SLOTS]

    def pair_copy(d):
        return send(
            gram_ref.at[chip_after(d), other_rows],
            pair.at[d],
            pair_send.at[d],
            pair_recv.at[d],
            {"lat": partner},
        )

    def lat_copy(d):
        return send(
            summed.at[d],
            got.at[d],
            lat_send.at[d],
            lat_recv.at[d],
            {"lat": chip_after(d) * 2 + core},
        )

    def begin(d):
        add_up(chip_after(d))
        pair_copy(d).start()


    def forward(d):
        pair_copy(d).wait_recv()
        summed[d] = gram_ref[chip_after(d), rows, :] + pair[d]
        lat_copy(d).start()

    def begin_and_forward(d):
        begin(d)
        forward(d - lag)

    lag = min(3, chips - 1)
    each(1, 1 + lag, begin)
    each(1 + lag, chips, begin_and_forward)
    begin(0)
    each(chips - lag, chips, forward)
    pair_copy(0).wait_recv()
    own = gram_ref[chip, rows, :] + pair[0]

    def collect(d, total):
        lat_copy(d).wait_recv()
        return total + got[d]

    own_ref[...] = lax.fori_loop(1, chips, collect, own)

    def thin_copy(d):
        return send(
            own_ref.at[pl.ds(tile_of(z_after(d)), 8)],
            thin_got.at[d],
            thin_send.at[d],
            thin_recv.at[d],
            {"mem": z_after(d)},
        )

    each(1, members, lambda d: thin_copy(d).start())

    def thin_collect(d, total):
        thin_copy(d).wait_recv()
        return total + thin_got[d]

    tile = lax.fori_loop(1, members, thin_collect, own_ref[pl.ds(tile_of(z), 8), :])

    def tile_rows(member):
        return pl.ds(pl.multiple_of(core * half + tile_of(member), 8), 8)

    full[tile_rows(z), :] = tile

    def wide_copy(e, member):
        return send(
            full.at[tile_rows(member)],
            full.at[tile_rows(member)],
            wide_send.at[e],
            wide_recv.at[e],
            {"mem": z_after(2 * e)},
        )

    each(1, members // 2, lambda e: wide_copy(e, z).start())
    each(
        1, members // 2, lambda e: wide_copy(e, lax.rem(z + members - 2 * e, members)).wait_recv()
    )
    half_copy = send(
        full.at[rows], full.at[rows], half_send.at[0], half_recv.at[0], {"lat": partner}
    )
    half_arrival = send(
        full.at[other_rows], full.at[other_rows], half_send.at[0], half_recv.at[0], {"lat": partner}
    )
    half_copy.start()
    half_arrival.wait_recv()

    out_ref[chip] = inverse_root_of(full[...], (members - 1.0) * band_span(widths_ref[...], chip))

    def root_copy(d, owner):
        return send(
            out_ref.at[owner, rows],
            out_ref.at[owner, rows],
            root_send.at[d],
            root_recv.at[d],
            {"lat": chip_after(d) * 2 + core},
        )

    def pass_copy(d, which):
        return send(
            out_ref.at[chip_before(d), which],
            out_ref.at[chip_before(d), which],
            pass_send.at[d],
            pass_recv.at[d],
            {"lat": partner},
        )

    each(1, chips, lambda d: root_copy(d, chip).start())

    whiten(chip)

    def hand_over(d):
        root_copy(d, chip_before(d)).wait_recv()
        pass_copy(d, rows).start()

    def take_over(d):
        pass_copy(d, other_rows).wait_recv()
        whiten(chip_before(d))

    def both_ways(d):
        hand_over(d)
        take_over(d - 1)

    hand_over(1)
    each(2, chips, both_ways)
    take_over(chips - 1)
    for q in range(owned):
        result = jnp.dot(
            spread_ref[:MM], moved[q], preferred_element_type=jnp.float32
        ).astype(jnp.bfloat16)
        for r in range(2):
            white_ref[r, q] = result[:, LEVELS * r : LEVELS * (r + 1)]

    def finish(d):
        pass_copy(d, rows).wait_send()
        root_copy(d, chip).wait_send()
        lat_copy(d).wait_send()

    each(1, chips, finish)
    each(0, chips, lambda d: pair_copy(d).wait_send())
    each(1, 2 * chips, lambda d: wave_copy(d, lat).wait_send())
    each(1, members, lambda d: thin_copy(d).wait_send())
    each(1, members // 2, lambda e: wide_copy(e, z).wait_send())
    half_copy.wait_send()


def transformed(waves, owner_map, band_widths, latitudes, owned, side):
    devices, per_device = waves.shape[:2]
    chips = devices // 2
    members = lax.axis_size("mem")
    half = LEVELS // 2
    dma = pltpu.SemaphoreType.DMA
    lanes = (MM + 127) // 128 * 128
    stride = (per_device + 7) // 8 * 8
    counts = [devices, chips, chips, members, members // 2, 1, chips, chips]
    return pl.pallas_call(
        functools.partial(band_kernel, side, chips, members),
        out_shape=(
            jax.ShapeDtypeStruct((2, owned, MM, LEVELS), jnp.bfloat16),
            jax.ShapeDtypeStruct((chips, LEVELS, LEVELS), jnp.float32),
        ),
        in_specs=[pl.BlockSpec(memory_space=pltpu.VMEM)] * 7,
        out_specs=(pl.BlockSpec(memory_space=pltpu.VMEM),) * 2,
        scratch_shapes=[
            pltpu.VMEM((MM, *latitudes[0].shape), jnp.float32),
            pltpu.VMEM(latitudes[0].shape, jnp.float32),
            pltpu.VMEM((chips * SLOTS, lanes), jnp.bfloat16),
            pltpu.VMEM((lanes, chips * SLOTS), jnp.bfloat16),
            pltpu.VMEM(waves.shape, jnp.bfloat16),
            pltpu.VMEM(((devices + 1) * stride, LEVELS), jnp.float32),
            pltpu.VMEM((owned, chips * SLOTS, 2 * LEVELS), jnp.bfloat16),
            pltpu.VMEM((owned, chips * SLOTS, 2 * LEVELS), jnp.bfloat16),
            pltpu.VMEM((chips, LEVELS, LEVELS), jnp.float32),
            pltpu.VMEM((chips, half, LEVELS), jnp.float32),
            pltpu.VMEM((chips, half, LEVELS), jnp.float32),
            pltpu.VMEM((chips, half, LEVELS), jnp.float32),
            pltpu.VMEM((half, LEVELS), jnp.float32),
            pltpu.VMEM((members, 8, LEVELS), jnp.float32),
            pltpu.VMEM((LEVELS, LEVELS), jnp.float32),
        ]
        + [dma((count,)) for count in counts for way in range(2)],
        compiler_params=pltpu.CompilerParams(
            collective_id=0, has_side_effects=True, vmem_limit_bytes=48 * 2**20
        ),
    )(waves, owner_map[None], band_widths[None], *latitudes)


def body(perturbation, owner_map, band_widths):
    lat_rows = perturbation.shape[1]
    lat_devices = lax.axis_size("lat")
    owned = MM // lat_devices
    wave_table = fourier_table(owner_map, NLON).reshape(2, lat_devices, owned, NLON)
    waves = jnp.einsum(
        "rdqk,jkl->drqjl", wave_table, perturbation[0], preferred_element_type=jnp.float32
    ).astype(jnp.bfloat16)
    waves = waves.reshape(lat_devices, 2 * owned * lat_rows, LEVELS)
    latitudes = latitude_rows(lat_rows * lat_devices, lat_rows)
    whitened, inverse_root = transformed(
        waves, owner_map, band_widths, latitudes, owned, CHIP_SIDE
    )
    return (whitened[None], inverse_root)


def solution(mesh):
    in_specs = (P("mem", "lat", None, None), P(), P())
    out_specs = (P("mem", None, "lat", None, None), P())
    return jax.shard_map(body, mesh=mesh, in_specs=in_specs, out_specs=out_specs, check_vma=False)
```

```python
import functools

import jax
import jax.numpy as jnp
import numpy as np
from jax import lax
from jax.experimental import pallas as pl
from jax.experimental.pallas import tpu as pltpu
from jax.sharding import PartitionSpec as P

NLAT = 160
NLON = 320
MM = 160
LEVELS = 128
BANDS = 16
NS_ITERS = 6
CHIP_SIDE = 4
SLOTS = 32

shrink_weight = 0.2


def legendre_rows(zonal, start_ref, cosine_ref, weight_ref, rows_ref):
    zonal_square = zonal * zonal
    lanes = start_ref.shape[1] // 128
    start = [start_ref[:, 128 * c : 128 * (c + 1)] for c in range(lanes)]
    cosine = [cosine_ref[:, 128 * c : 128 * (c + 1)] for c in range(lanes)]
    weight = [weight_ref[:, 128 * c : 128 * (c + 1)] for c in range(lanes)]

    def advance(step, carry):
        for inner in range(8):
            index = step * 8 + inner
            degree = index.astype(jnp.float32)
            is_above = degree > zonal
            is_equal = degree == zonal
            upper_coef = jnp.sqrt(
                jnp.maximum(4.0 * degree * degree - 1.0, 1.0)
                / jnp.where(is_above, degree * degree - zonal_square, 1.0)
            )
            lower = degree - 1.0
            lower_coef = jnp.sqrt(
                jnp.maximum(lower * lower - zonal_square, 0.0)
                / jnp.maximum(4.0 * lower * lower - 1.0, 1.0)
            )
            following = []
            for c in range(lanes):
                previous, earlier = carry[2 * c], carry[2 * c + 1]
                climbed = upper_coef * (cosine[c] * previous - lower_coef * earlier)
                current = jnp.where(is_above, climbed, jnp.where(is_equal, start[c], 0.0))
                rows_ref[index, :, 128 * c : 128 * (c + 1)] = current * weight[c]
                following += [current, previous]
            carry = tuple(following)
        return carry

    zero = jnp.zeros_like(zonal)
    lax.fori_loop(0, MM // 8, advance, (zero,) * (2 * lanes))


def latitude_rows(lat_count, lat_rows):
    rows, lanes = 8, (max(lat_count, MM) + 127) // 128 * 128
    devices = lat_count // lat_rows
    place = np.arange(lat_count)
    colatitude = np.pi * (place % devices * lat_rows + place // devices + 0.5) / lat_count
    counter = np.arange(1, MM + 1)
    log_ratio = np.log((2.0 * counter - 1.0) / (2.0 * counter))

    def spread(row):
        return np.tile(np.pad(row, (0, lanes - row.size)).astype(np.float32), (rows, 1))

    sine = np.sin(colatitude)
    weight = np.sqrt(np.pi / lat_count) * sine
    return (spread(log_ratio), spread(np.log(sine)), spread(np.cos(colatitude)), spread(weight))


def owned_orders(owner, first):
    rows, count = 8, owner.shape[1]
    row = lax.broadcasted_iota(jnp.int32, (rows, count), 0)
    place = lax.broadcasted_iota(jnp.int32, (rows, count), 1)
    held = jnp.broadcast_to(owner.astype(jnp.float32), (rows, count))
    return jnp.sum(jnp.where(place == first + row, held, 0.0), axis=1, keepdims=True)


def first_values(orders, log_ratio, log_sine):
    counter = lax.broadcasted_iota(jnp.int32, log_ratio.shape, 1).astype(jnp.float32) + 1.0
    log_factor = jnp.sum(jnp.where(counter <= orders, log_ratio, 0.0), axis=1, keepdims=True)
    log_norm = 0.5 * jnp.log((2.0 * orders + 1.0) / 2.0) + 0.5 * log_factor
    return jnp.exp(log_norm + orders * log_sine)


def slot_selectors(widths, bands, total):
    slots, lanes = bands * SLOTS, widths.shape[1]
    wide = widths.astype(jnp.float32)
    band = lax.broadcasted_iota(jnp.int32, (slots, lanes), 0) // SLOTS
    other = lax.broadcasted_iota(jnp.int32, (slots, lanes), 1)
    rows = jnp.broadcast_to(wide, (slots, lanes))
    start = jnp.sum(jnp.where(other < band, rows, 0.0), axis=1, keepdims=True)
    width = jnp.sum(jnp.where(other == band, rows, 0.0), axis=1, keepdims=True)
    place = (lax.broadcasted_iota(jnp.int32, (slots, 1), 0) % SLOTS).astype(jnp.float32)
    degree = jnp.where(place < width, start + place, -1.0)
    row = lax.broadcasted_iota(jnp.int32, (slots, total), 1).astype(jnp.float32)
    return jnp.where(degree == row, 1.0, 0.0)


def band_span(widths, band):
    other = lax.broadcasted_iota(jnp.int32, widths.shape, 1)
    wide = widths.astype(jnp.float32)
    start = jnp.sum(jnp.where(other < band, wide, 0.0), axis=1, keepdims=True)
    end = jnp.sum(jnp.where(other <= band, wide, 0.0), axis=1, keepdims=True)
    return end * end - start * start


def fourier_table(orders, lon_count):
    phases = np.arange(MM)[:, None] * np.arange(lon_count)[None, :] % lon_count
    angles = phases * (2.0 * np.pi / lon_count)
    scaling = np.sqrt(2.0 / lon_count)
    waves = np.stack([scaling * np.cos(angles), -scaling * np.sin(angles)])
    waves = jnp.asarray(waves.astype(np.float32)).astype(jnp.bfloat16)
    pick = (orders[:, None] == jnp.arange(MM, dtype=jnp.int32)[None, :]).astype(jnp.bfloat16)
    return jnp.einsum(
        "pm,rmk->rpk", pick, waves, preferred_element_type=jnp.float32
    ).astype(jnp.bfloat16)


def inverse_root_of(gram, denominator):
    row = lax.broadcasted_iota(jnp.int32, (LEVELS, LEVELS), 0)
    column = lax.broadcasted_iota(jnp.int32, (LEVELS, LEVELS), 1)
    identity = (row == column).astype(jnp.float32)

    def whole_sum(array):
        return jnp.sum(jnp.sum(array, axis=0, keepdims=True), axis=1, keepdims=True)

    def pieces(array):
        first = array.astype(jnp.bfloat16)
        rest = array - first.astype(jnp.float32)
        second = rest.astype(jnp.bfloat16)
        third = (rest - second.astype(jnp.float32)).astype(jnp.bfloat16)
        return (first, second, third)

    def product(left, right):
        a, b = pieces(left), pieces(right)
        terms = ((0, 2), (1, 1), (2, 0), (0, 1), (1, 0), (0, 0))
        return jnp.dot(
            jnp.concatenate([a[i] for i, j in terms], axis=1),
            jnp.concatenate([b[j] for i, j in terms], axis=0),
            preferred_element_type=jnp.float32,
        )

    covariance = gram / denominator
    spread = whole_sum(covariance * identity) / LEVELS
    shrunk = (1.0 - shrink_weight) * covariance + shrink_weight * spread * identity
    frobenius = jnp.sqrt(whole_sum(shrunk * shrunk) + 1e-06)
    growing = shrunk / frobenius
    inverse = 1.5 * identity - 0.5 * growing
    growing = product(growing, inverse)
    for iteration in range(NS_ITERS - 1):
        middle = 1.5 * identity - 0.5 * product(inverse, growing)
        if iteration < NS_ITERS - 2:
            growing = product(growing, middle)
        inverse = product(middle, inverse)
    return inverse / jnp.sqrt(frobenius)


def band_kernel(
    side,
    chips,
    members,
    waves_ref,
    owner_ref,
    widths_ref,
    ratio_ref,
    sine_ref,
    cosine_ref,
    weight_ref,
    white_ref,
    out_ref,
    rows_ref,
    start_ref,
    select_ref,
    spread_ref,
    arrived,
    grid,
    masked,
    moved,
    gram_ref,
    pair,
    summed,
    got,
    own_ref,
    thin_got,
    full,
    wave_send,
    wave_recv,
    pair_send,
    pair_recv,
    lat_send,
    lat_recv,
    thin_send,
    thin_recv,
    wide_send,
    wide_recv,
    half_send,
    half_recv,
    root_send,
    root_recv,
    pass_send,
    pass_recv,
):
    lat = lax.axis_index("lat")
    z = lax.axis_index("mem")
    core = lax.rem(lat, 2)
    chip = lax.div(lat, 2)
    partner = chip * 2 + 1 - core
    half = LEVELS // 2
    rows = pl.ds(pl.multiple_of(core * half, half), half)
    other_rows = pl.ds(pl.multiple_of((1 - core) * half, half), half)
    wide = chips // side

    def chip_after(d):
        x = lax.rem(lax.div(chip, side) + lax.div(d, side), wide)
        y = lax.rem(lax.rem(chip, side) + lax.rem(d, side), side)
        return x * side + y

    def chip_before(d):
        x = lax.rem(lax.div(chip, side) + wide - lax.div(d, side), wide)
        y = lax.rem(lax.rem(chip, side) + side - lax.rem(d, side), side)
        return x * side + y

    def lat_after(d):
        return chip_after(lax.div(d, 2)) * 2 + lax.rem(core + lax.rem(d, 2), 2)

    def lat_before(d):
        return chip_before(lax.div(d, 2)) * 2 + lax.rem(core + lax.rem(d, 2), 2)

    def z_after(d):
        return lax.rem(z + d, members)

    def tile_of(member):
        return pl.multiple_of(lax.div(member, 2) * 8, 8)

    def send(source, target, send_sem, recv_sem, device):
        return pltpu.make_async_remote_copy(
            src_ref=source,
            dst_ref=target,
            send_sem=send_sem,
            recv_sem=recv_sem,
            device_id=device,
            device_id_type=pl.DeviceIdType.MESH,
        )

    def each(first, last, work):
        def step(d, carry):
            work(d)
            return carry

        lax.fori_loop(first, last, step, 0)

    barrier = pltpu.get_barrier_semaphore()

    def greet(device):
        pl.semaphore_signal(
            barrier, inc=1, device_id=device, device_id_type=pl.DeviceIdType.MESH
        )

    each(1, members, lambda d: greet({"mem": z_after(d)}))
    each(1, 2 * chips, lambda d: greet({"lat": lat_after(d)}))
    orders = owned_orders(owner_ref[...], lat * masked.shape[0])
    start_ref[...] = first_values(orders, ratio_ref[...], sine_ref[...])
    zonal = jnp.broadcast_to(orders, (orders.shape[0], 128))
    select = slot_selectors(widths_ref[...], chips, select_ref.shape[1])
    select_ref[...] = select.astype(jnp.bfloat16)
    spread_ref[...] = jnp.transpose(select).astype(jnp.bfloat16)
    legendre_rows(zonal, start_ref, cosine_ref, weight_ref, rows_ref)
    pl.semaphore_wait(barrier, members - 1 + 2 * chips - 1)

    def wave_copy(d, source):
        return send(
            waves_ref.at[lat_after(d)],
            arrived.at[source],
            wave_send.at[d],
            wave_recv.at[d],
            {"lat": lat_after(d)},
        )

    each(1, 2 * chips, lambda d: wave_copy(d, lat).start())
    arrived[lat] = waves_ref[lat]
    each(1, 2 * chips, lambda d: wave_copy(d, lat_before(d)).wait_recv())
    devices, per_device = arrived.shape[0], arrived.shape[1]
    owned = masked.shape[0]
    lat_rows = per_device // (2 * owned)
    stride = grid.shape[0] // (devices + 1)
    for device in range(devices):
        grid[device * stride : device * stride + per_device] = arrived[device].astype(jnp.float32)

    def field(r, q):
        first = (r * owned + q) * lat_rows
        parts = [grid[pl.ds(first + k, devices, stride=stride), :] for k in range(lat_rows)]
        return jnp.concatenate(parts, axis=0)

    for q in range(owned):
        table = rows_ref[:, q, :][:, : devices * lat_rows].astype(jnp.bfloat16)
        both = jnp.concatenate([field(0, q), field(1, q)], axis=1).astype(jnp.bfloat16)
        coefficients = jnp.dot(table, both, preferred_element_type=jnp.float32)
        masked[q] = jnp.dot(
            select_ref[:, :MM],
            coefficients.astype(jnp.bfloat16),
            preferred_element_type=jnp.float32,
        ).astype(jnp.bfloat16)

    def band_slots(band):
        return pl.ds(pl.multiple_of(band * SLOTS, SLOTS), SLOTS)

    def band_values(band):
        slots = band_slots(band)
        return jnp.concatenate(
            [
                masked[q, slots, LEVELS * r : LEVELS * (r + 1)]
                for q in range(owned)
                for r in range(2)
            ],
            axis=0,
        )

    def add_up(band):
        values = band_values(band)
        gram_ref[band] = lax.dot_general(
            values, values, (((0,), (0,)), ((), ())), preferred_element_type=jnp.float32
        )

    def whiten(band):
        root_low = out_ref[band].astype(jnp.bfloat16)
        turned = lax.dot_general(
            band_values(band),
            root_low,
            (((1,), (1,)), ((), ())),
            preferred_element_type=jnp.float32,
        ).astype(jnp.bfloat16)
        slots = band_slots(band)
        for q in range(owned):
            for r in range(2):
                row = (2 * q + r) * SLOTS
                moved[q, slots, LEVELS * r : LEVELS * (r + 1)] = turned[row : row + SLOTS]

    def pair_copy(d):
        return send(
            gram_ref.at[chip_after(d), other_rows],
            pair.at[d],
            pair_send.at[d],
            pair_recv.at[d],
            {"lat": partner},
        )

    def lat_copy(d):
        return send(
            summed.at[d],
            got.at[d],
            lat_send.at[d],
            lat_recv.at[d],
            {"lat": chip_after(d) * 2 + core},
        )

    def begin(d):
        add_up(chip_after(d))
        pair_copy(d).start()


    def forward(d):
        pair_copy(d).wait_recv()
        summed[d] = gram_ref[chip_after(d), rows, :] + pair[d]
        lat_copy(d).start()

    def begin_and_forward(d):
        begin(d)
        forward(d - lag)

    lag = min(3, chips - 1)
    each(1, 1 + lag, begin)
    each(1 + lag, chips, begin_and_forward)
    begin(0)
    each(chips - lag, chips, forward)
    pair_copy(0).wait_recv()
    own = gram_ref[chip, rows, :] + pair[0]

    def collect(d, total):
        lat_copy(d).wait_recv()
        return total + got[d]

    own_ref[...] = lax.fori_loop(1, chips, collect, own)

    def thin_copy(d):
        return send(
            own_ref.at[pl.ds(tile_of(z_after(d)), 8)],
            thin_got.at[d],
            thin_send.at[d],
            thin_recv.at[d],
            {"mem": z_after(d)},
        )

    each(1, members, lambda d: thin_copy(d).start())

    def thin_collect(d, total):
        thin_copy(d).wait_recv()
        return total + thin_got[d]

    tile = lax.fori_loop(1, members, thin_collect, own_ref[pl.ds(tile_of(z), 8), :])

    def tile_rows(member):
        return pl.ds(pl.multiple_of(core * half + tile_of(member), 8), 8)

    full[tile_rows(z), :] = tile

    def wide_copy(e, member):
        return send(
            full.at[tile_rows(member)],
            full.at[tile_rows(member)],
            wide_send.at[e],
            wide_recv.at[e],
            {"mem": z_after(2 * e)},
        )

    each(1, members // 2, lambda e: wide_copy(e, z).start())
    each(
        1, members // 2, lambda e: wide_copy(e, lax.rem(z + members - 2 * e, members)).wait_recv()
    )
    half_copy = send(
        full.at[rows], full.at[rows], half_send.at[0], half_recv.at[0], {"lat": partner}
    )
    half_arrival = send(
        full.at[other_rows], full.at[other_rows], half_send.at[0], half_recv.at[0], {"lat": partner}
    )
    half_copy.start()
    half_arrival.wait_recv()

    out_ref[chip] = inverse_root_of(full[...], (members - 1.0) * band_span(widths_ref[...], chip))

    def root_copy(d, owner):
        return send(
            out_ref.at[owner, rows],
            out_ref.at[owner, rows],
            root_send.at[d],
            root_recv.at[d],
            {"lat": chip_after(d) * 2 + core},
        )

    def pass_copy(d, which):
        return send(
            out_ref.at[chip_before(d), which],
            out_ref.at[chip_before(d), which],
            pass_send.at[d],
            pass_recv.at[d],
            {"lat": partner},
        )

    each(1, chips, lambda d: root_copy(d, chip).start())

    whiten(chip)

    def hand_over(d):
        root_copy(d, chip_before(d)).wait_recv()
        pass_copy(d, rows).start()

    def take_over(d):
        pass_copy(d, other_rows).wait_recv()
        whiten(chip_before(d))

    def both_ways(d):
        hand_over(d)
        take_over(d - 1)

    hand_over(1)
    each(2, chips, both_ways)
    take_over(chips - 1)
    for q in range(owned):
        result = jnp.dot(
            spread_ref[:MM], moved[q], preferred_element_type=jnp.float32
        ).astype(jnp.bfloat16)
        for r in range(2):
            white_ref[r, q] = result[:, LEVELS * r : LEVELS * (r + 1)]

    def finish(d):
        pass_copy(d, rows).wait_send()
        root_copy(d, chip).wait_send()
        lat_copy(d).wait_send()

    each(1, chips, finish)
    each(0, chips, lambda d: pair_copy(d).wait_send())
    each(1, 2 * chips, lambda d: wave_copy(d, lat).wait_send())
    each(1, members, lambda d: thin_copy(d).wait_send())
    each(1, members // 2, lambda e: wide_copy(e, z).wait_send())
    half_copy.wait_send()


def transformed(waves, owner_map, band_widths, latitudes, owned, side):
    devices, per_device = waves.shape[:2]
    chips = devices // 2
    members = lax.axis_size("mem")
    half = LEVELS // 2
    dma = pltpu.SemaphoreType.DMA
    lanes = (MM + 127) // 128 * 128
    stride = (per_device + 7) // 8 * 8
    counts = [devices, chips, chips, members, members // 2, 1, chips, chips]
    return pl.pallas_call(
        functools.partial(band_kernel, side, chips, members),
        out_shape=(
            jax.ShapeDtypeStruct((2, owned, MM, LEVELS), jnp.bfloat16),
            jax.ShapeDtypeStruct((chips, LEVELS, LEVELS), jnp.float32),
        ),
        in_specs=[pl.BlockSpec(memory_space=pltpu.VMEM)] * 7,
        out_specs=(pl.BlockSpec(memory_space=pltpu.VMEM),) * 2,
        scratch_shapes=[
            pltpu.VMEM((MM, *latitudes[0].shape), jnp.float32),
            pltpu.VMEM(latitudes[0].shape, jnp.float32),
            pltpu.VMEM((chips * SLOTS, lanes), jnp.bfloat16),
            pltpu.VMEM((lanes, chips * SLOTS), jnp.bfloat16),
            pltpu.VMEM(waves.shape, jnp.bfloat16),
            pltpu.VMEM(((devices + 1) * stride, LEVELS), jnp.float32),
            pltpu.VMEM((owned, chips * SLOTS, 2 * LEVELS), jnp.bfloat16),
            pltpu.VMEM((owned, chips * SLOTS, 2 * LEVELS), jnp.bfloat16),
            pltpu.VMEM((chips, LEVELS, LEVELS), jnp.float32),
            pltpu.VMEM((chips, half, LEVELS), jnp.float32),
            pltpu.VMEM((chips, half, LEVELS), jnp.float32),
            pltpu.VMEM((chips, half, LEVELS), jnp.float32),
            pltpu.VMEM((half, LEVELS), jnp.float32),
            pltpu.VMEM((members, 8, LEVELS), jnp.float32),
            pltpu.VMEM((LEVELS, LEVELS), jnp.float32),
        ]
        + [dma((count,)) for count in counts for way in range(2)],
        compiler_params=pltpu.CompilerParams(
            collective_id=0, has_side_effects=True, vmem_limit_bytes=48 * 2**20
        ),
    )(waves, owner_map[None], band_widths[None], *latitudes)


def body(perturbation, owner_map, band_widths):
    lat_rows = perturbation.shape[1]
    lat_devices = lax.axis_size("lat")
    owned = MM // lat_devices
    wave_table = fourier_table(owner_map, NLON).reshape(2, lat_devices, owned, NLON)
    waves = jnp.einsum(
        "rdqk,jkl->drqjl", wave_table, perturbation[0], preferred_element_type=jnp.float32
    ).astype(jnp.bfloat16)
    waves = waves.reshape(lat_devices, 2 * owned * lat_rows, LEVELS)
    latitudes = latitude_rows(lat_rows * lat_devices, lat_rows)
    whitened, inverse_root = transformed(
        waves, owner_map, band_widths, latitudes, owned, CHIP_SIDE
    )
    return (whitened[None], inverse_root)


def solution(mesh):
    in_specs = (P("mem", "lat", None, None), P(), P())
    out_specs = (P("mem", None, "lat", None, None), P())
    return jax.shard_map(body, mesh=mesh, in_specs=in_specs, out_specs=out_specs, check_vma=False)
```

```python
import functools

import jax
import jax.numpy as jnp
import numpy as np
from jax import lax
from jax.experimental import pallas as pl
from jax.experimental.pallas import tpu as pltpu
from jax.sharding import PartitionSpec as P

NLAT = 160
NLON = 320
MM = 160
LEVELS = 128
BANDS = 16
NS_ITERS = 6
CHIP_SIDE = 4
SLOTS = 32

shrink_weight = 0.2


def legendre_rows(zonal, start_ref, cosine_ref, weight_ref, rows_ref):
    zonal_square = zonal * zonal
    lanes = start_ref.shape[1] // 128
    start = [start_ref[:, 128 * c : 128 * (c + 1)] for c in range(lanes)]
    cosine = [cosine_ref[:, 128 * c : 128 * (c + 1)] for c in range(lanes)]
    weight = [weight_ref[:, 128 * c : 128 * (c + 1)] for c in range(lanes)]

    def advance(step, carry):
        for inner in range(8):
            index = step * 8 + inner
            degree = index.astype(jnp.float32)
            is_above = degree > zonal
            is_equal = degree == zonal
            upper_coef = jnp.sqrt(
                jnp.maximum(4.0 * degree * degree - 1.0, 1.0)
                / jnp.where(is_above, degree * degree - zonal_square, 1.0)
            )
            lower = degree - 1.0
            lower_coef = jnp.sqrt(
                jnp.maximum(lower * lower - zonal_square, 0.0)
                / jnp.maximum(4.0 * lower * lower - 1.0, 1.0)
            )
            following = []
            for c in range(lanes):
                previous, earlier = carry[2 * c], carry[2 * c + 1]
                climbed = upper_coef * (cosine[c] * previous - lower_coef * earlier)
                current = jnp.where(is_above, climbed, jnp.where(is_equal, start[c], 0.0))
                rows_ref[index, :, 128 * c : 128 * (c + 1)] = current * weight[c]
                following += [current, previous]
            carry = tuple(following)
        return carry

    zero = jnp.zeros_like(zonal)
    lax.fori_loop(0, MM // 8, advance, (zero,) * (2 * lanes))


def latitude_rows(lat_count, lat_rows):
    rows, lanes = 8, (max(lat_count, MM) + 127) // 128 * 128
    devices = lat_count // lat_rows
    place = np.arange(lat_count)
    colatitude = np.pi * (place % devices * lat_rows + place // devices + 0.5) / lat_count
    counter = np.arange(1, MM + 1)
    log_ratio = np.log((2.0 * counter - 1.0) / (2.0 * counter))

    def spread(row):
        return np.tile(np.pad(row, (0, lanes - row.size)).astype(np.float32), (rows, 1))

    sine = np.sin(colatitude)
    weight = np.sqrt(np.pi / lat_count) * sine
    return (spread(log_ratio), spread(np.log(sine)), spread(np.cos(colatitude)), spread(weight))


def owned_orders(owner, first):
    rows, count = 8, owner.shape[1]
    row = lax.broadcasted_iota(jnp.int32, (rows, count), 0)
    place = lax.broadcasted_iota(jnp.int32, (rows, count), 1)
    held = jnp.broadcast_to(owner.astype(jnp.float32), (rows, count))
    return jnp.sum(jnp.where(place == first + row, held, 0.0), axis=1, keepdims=True)


def first_values(orders, log_ratio, log_sine):
    counter = lax.broadcasted_iota(jnp.int32, log_ratio.shape, 1).astype(jnp.float32) + 1.0
    log_factor = jnp.sum(jnp.where(counter <= orders, log_ratio, 0.0), axis=1, keepdims=True)
    log_norm = 0.5 * jnp.log((2.0 * orders + 1.0) / 2.0) + 0.5 * log_factor
    return jnp.exp(log_norm + orders * log_sine)


def slot_selectors(widths, bands, total):
    slots, lanes = bands * SLOTS, widths.shape[1]
    wide = widths.astype(jnp.float32)
    band = lax.broadcasted_iota(jnp.int32, (slots, lanes), 0) // SLOTS
    other = lax.broadcasted_iota(jnp.int32, (slots, lanes), 1)
    rows = jnp.broadcast_to(wide, (slots, lanes))
    start = jnp.sum(jnp.where(other < band, rows, 0.0), axis=1, keepdims=True)
    width = jnp.sum(jnp.where(other == band, rows, 0.0), axis=1, keepdims=True)
    place = (lax.broadcasted_iota(jnp.int32, (slots, 1), 0) % SLOTS).astype(jnp.float32)
    degree = jnp.where(place < width, start + place, -1.0)
    row = lax.broadcasted_iota(jnp.int32, (slots, total), 1).astype(jnp.float32)
    return jnp.where(degree == row, 1.0, 0.0)


def band_span(widths, band):
    other = lax.broadcasted_iota(jnp.int32, widths.shape, 1)
    wide = widths.astype(jnp.float32)
    start = jnp.sum(jnp.where(other < band, wide, 0.0), axis=1, keepdims=True)
    end = jnp.sum(jnp.where(other <= band, wide, 0.0), axis=1, keepdims=True)
    return end * end - start * start


def fourier_table(orders, lon_count):
    phases = np.arange(MM)[:, None] * np.arange(lon_count)[None, :] % lon_count
    angles = phases * (2.0 * np.pi / lon_count)
    scaling = np.sqrt(2.0 / lon_count)
    waves = np.stack([scaling * np.cos(angles), -scaling * np.sin(angles)])
    waves = jnp.asarray(waves.astype(np.float32)).astype(jnp.bfloat16)
    pick = (orders[:, None] == jnp.arange(MM, dtype=jnp.int32)[None, :]).astype(jnp.bfloat16)
    return jnp.einsum(
        "pm,rmk->rpk", pick, waves, preferred_element_type=jnp.float32
    ).astype(jnp.bfloat16)


def inverse_root_of(gram, denominator):
    row = lax.broadcasted_iota(jnp.int32, (LEVELS, LEVELS), 0)
    column = lax.broadcasted_iota(jnp.int32, (LEVELS, LEVELS), 1)
    identity = (row == column).astype(jnp.float32)

    def whole_sum(array):
        return jnp.sum(jnp.sum(array, axis=0, keepdims=True), axis=1, keepdims=True)

    def pieces(array):
        first = array.astype(jnp.bfloat16)
        rest = array - first.astype(jnp.float32)
        second = rest.astype(jnp.bfloat16)
        third = (rest - second.astype(jnp.float32)).astype(jnp.bfloat16)
        return (first, second, third)

    def product(left, right):
        a, b = pieces(left), pieces(right)
        terms = ((0, 2), (1, 1), (2, 0), (0, 1), (1, 0), (0, 0))
        return jnp.dot(
            jnp.concatenate([a[i] for i, j in terms], axis=1),
            jnp.concatenate([b[j] for i, j in terms], axis=0),
            preferred_element_type=jnp.float32,
        )

    covariance = gram / denominator
    spread = whole_sum(covariance * identity) / LEVELS
    shrunk = (1.0 - shrink_weight) * covariance + shrink_weight * spread * identity
    frobenius = jnp.sqrt(whole_sum(shrunk * shrunk) + 1e-06)
    growing = shrunk / frobenius
    inverse = 1.5 * identity - 0.5 * growing
    growing = product(growing, inverse)
    for iteration in range(NS_ITERS - 1):
        middle = 1.5 * identity - 0.5 * product(inverse, growing)
        if iteration < NS_ITERS - 2:
            growing = product(growing, middle)
        inverse = product(middle, inverse)
    return inverse / jnp.sqrt(frobenius)


def band_kernel(
    side,
    chips,
    members,
    waves_ref,
    owner_ref,
    widths_ref,
    ratio_ref,
    sine_ref,
    cosine_ref,
    weight_ref,
    white_ref,
    out_ref,
    rows_ref,
    start_ref,
    select_ref,
    spread_ref,
    arrived,
    grid,
    masked,
    moved,
    gram_ref,
    pair,
    summed,
    got,
    own_ref,
    thin_got,
    full,
    wave_send,
    wave_recv,
    pair_send,
    pair_recv,
    lat_send,
    lat_recv,
    thin_send,
    thin_recv,
    wide_send,
    wide_recv,
    half_send,
    half_recv,
    root_send,
    root_recv,
    pass_send,
    pass_recv,
):
    lat = lax.axis_index("lat")
    z = lax.axis_index("mem")
    core = lax.rem(lat, 2)
    chip = lax.div(lat, 2)
    partner = chip * 2 + 1 - core
    half = LEVELS // 2
    rows = pl.ds(pl.multiple_of(core * half, half), half)
    other_rows = pl.ds(pl.multiple_of((1 - core) * half, half), half)
    wide = chips // side

    def chip_after(d):
        x = lax.rem(lax.div(chip, side) + lax.div(d, side), wide)
        y = lax.rem(lax.rem(chip, side) + lax.rem(d, side), side)
        return x * side + y

    def chip_before(d):
        x = lax.rem(lax.div(chip, side) + wide - lax.div(d, side), wide)
        y = lax.rem(lax.rem(chip, side) + side - lax.rem(d, side), side)
        return x * side + y

    def lat_after(d):
        return chip_after(lax.div(d, 2)) * 2 + lax.rem(core + lax.rem(d, 2), 2)

    def lat_before(d):
        return chip_before(lax.div(d, 2)) * 2 + lax.rem(core + lax.rem(d, 2), 2)

    def z_after(d):
        return lax.rem(z + d, members)

    def tile_of(member):
        return pl.multiple_of(lax.div(member, 2) * 8, 8)

    def send(source, target, send_sem, recv_sem, device):
        return pltpu.make_async_remote_copy(
            src_ref=source,
            dst_ref=target,
            send_sem=send_sem,
            recv_sem=recv_sem,
            device_id=device,
            device_id_type=pl.DeviceIdType.MESH,
        )

    def each(first, last, work):
        def step(d, carry):
            work(d)
            return carry

        lax.fori_loop(first, last, step, 0)

    barrier = pltpu.get_barrier_semaphore()

    def greet(device):
        pl.semaphore_signal(
            barrier, inc=1, device_id=device, device_id_type=pl.DeviceIdType.MESH
        )

    each(1, members, lambda d: greet({"mem": z_after(d)}))
    each(1, 2 * chips, lambda d: greet({"lat": lat_after(d)}))
    orders = owned_orders(owner_ref[...], lat * masked.shape[0])
    start_ref[...] = first_values(orders, ratio_ref[...], sine_ref[...])
    zonal = jnp.broadcast_to(orders, (orders.shape[0], 128))
    select = slot_selectors(widths_ref[...], chips, select_ref.shape[1])
    select_ref[...] = select.astype(jnp.bfloat16)
    spread_ref[...] = jnp.transpose(select).astype(jnp.bfloat16)
    pl.semaphore_wait(barrier, members - 1 + 2 * chips - 1)

    def wave_copy(d, source):
        return send(
            waves_ref.at[lat_after(d)],
            arrived.at[source],
            wave_send.at[d],
            wave_recv.at[d],
            {"lat": lat_after(d)},
        )

    each(1, 2 * chips, lambda d: wave_copy(d, lat).start())
    arrived[lat] = waves_ref[lat]
    legendre_rows(zonal, start_ref, cosine_ref, weight_ref, rows_ref)
    each(1, 2 * chips, lambda d: wave_copy(d, lat_before(d)).wait_recv())
    devices, per_device = arrived.shape[0], arrived.shape[1]
    owned = masked.shape[0]
    lat_rows = per_device // (2 * owned)
    stride = grid.shape[0] // (devices + 1)
    for device in range(devices):
        grid[device * stride : device * stride + per_device] = arrived[device].astype(jnp.float32)

    def field(r, q):
        first = (r * owned + q) * lat_rows
        parts = [grid[pl.ds(first + k, devices, stride=stride), :] for k in range(lat_rows)]
        return jnp.concatenate(parts, axis=0)

    for q in range(owned):
        table = rows_ref[:, q, :][:, : devices * lat_rows].astype(jnp.bfloat16)
        both = jnp.concatenate([field(0, q), field(1, q)], axis=1).astype(jnp.bfloat16)
        coefficients = jnp.dot(table, both, preferred_element_type=jnp.float32)
        masked[q] = jnp.dot(
            select_ref[:, :MM],
            coefficients.astype(jnp.bfloat16),
            preferred_element_type=jnp.float32,
        ).astype(jnp.bfloat16)

    def band_slots(band):
        return pl.ds(pl.multiple_of(band * SLOTS, SLOTS), SLOTS)

    def band_values(band):
        slots = band_slots(band)
        return jnp.concatenate(
            [
                masked[q, slots, LEVELS * r : LEVELS * (r + 1)]
                for q in range(owned)
                for r in range(2)
            ],
            axis=0,
        )

    def add_up(band):
        values = band_values(band)
        gram_ref[band] = lax.dot_general(
            values, values, (((0,), (0,)), ((), ())), preferred_element_type=jnp.float32
        )

    def whiten(band):
        root_low = out_ref[band].astype(jnp.bfloat16)
        turned = lax.dot_general(
            band_values(band),
            root_low,
            (((1,), (1,)), ((), ())),
            preferred_element_type=jnp.float32,
        ).astype(jnp.bfloat16)
        slots = band_slots(band)
        for q in range(owned):
            for r in range(2):
                row = (2 * q + r) * SLOTS
                moved[q, slots, LEVELS * r : LEVELS * (r + 1)] = turned[row : row + SLOTS]

    def pair_copy(d):
        return send(
            gram_ref.at[chip_after(d), other_rows],
            pair.at[d],
            pair_send.at[d],
            pair_recv.at[d],
            {"lat": partner},
        )

    def lat_copy(d):
        return send(
            summed.at[d],
            got.at[d],
            lat_send.at[d],
            lat_recv.at[d],
            {"lat": chip_after(d) * 2 + core},
        )

    def begin(d):
        add_up(chip_after(d))
        pair_copy(d).start()


    def forward(d):
        pair_copy(d).wait_recv()
        summed[d] = gram_ref[chip_after(d), rows, :] + pair[d]
        lat_copy(d).start()

    def begin_and_forward(d):
        begin(d)
        forward(d - lag)

    lag = min(3, chips - 1)
    each(1, 1 + lag, begin)
    each(1 + lag, chips, begin_and_forward)
    begin(0)
    each(chips - lag, chips, forward)
    pair_copy(0).wait_recv()
    own = gram_ref[chip, rows, :] + pair[0]

    def collect(d, total):
        lat_copy(d).wait_recv()
        return total + got[d]

    own_ref[...] = lax.fori_loop(1, chips, collect, own)

    def thin_copy(d):
        return send(
            own_ref.at[pl.ds(tile_of(z_after(d)), 8)],
            thin_got.at[d],
            thin_send.at[d],
            thin_recv.at[d],
            {"mem": z_after(d)},
        )

    each(1, members, lambda d: thin_copy(d).start())

    def thin_collect(d, total):
        thin_copy(d).wait_recv()
        return total + thin_got[d]

    tile = lax.fori_loop(1, members, thin_collect, own_ref[pl.ds(tile_of(z), 8), :])

    def tile_rows(member):
        return pl.ds(pl.multiple_of(core * half + tile_of(member), 8), 8)

    full[tile_rows(z), :] = tile

    def wide_copy(e, member):
        return send(
            full.at[tile_rows(member)],
            full.at[tile_rows(member)],
            wide_send.at[e],
            wide_recv.at[e],
            {"mem": z_after(2 * e)},
        )

    each(1, members // 2, lambda e: wide_copy(e, z).start())
    each(
        1, members // 2, lambda e: wide_copy(e, lax.rem(z + members - 2 * e, members)).wait_recv()
    )
    half_copy = send(
        full.at[rows], full.at[rows], half_send.at[0], half_recv.at[0], {"lat": partner}
    )
    half_arrival = send(
        full.at[other_rows], full.at[other_rows], half_send.at[0], half_recv.at[0], {"lat": partner}
    )
    half_copy.start()
    half_arrival.wait_recv()

    out_ref[chip] = inverse_root_of(full[...], (members - 1.0) * band_span(widths_ref[...], chip))

    def root_copy(d, owner):
        return send(
            out_ref.at[owner, rows],
            out_ref.at[owner, rows],
            root_send.at[d],
            root_recv.at[d],
            {"lat": chip_after(d) * 2 + core},
        )

    def pass_copy(d, which):
        return send(
            out_ref.at[chip_before(d), which],
            out_ref.at[chip_before(d), which],
            pass_send.at[d],
            pass_recv.at[d],
            {"lat": partner},
        )

    each(1, chips, lambda d: root_copy(d, chip).start())

    whiten(chip)

    def hand_over(d):
        root_copy(d, chip_before(d)).wait_recv()
        pass_copy(d, rows).start()

    def take_over(d):
        pass_copy(d, other_rows).wait_recv()
        whiten(chip_before(d))

    def both_ways(d):
        hand_over(d)
        take_over(d - 1)

    hand_over(1)
    each(2, chips, both_ways)
    take_over(chips - 1)
    for q in range(owned):
        result = jnp.dot(
            spread_ref[:MM], moved[q], preferred_element_type=jnp.float32
        ).astype(jnp.bfloat16)
        for r in range(2):
            white_ref[r, q] = result[:, LEVELS * r : LEVELS * (r + 1)]

    def finish(d):
        pass_copy(d, rows).wait_send()
        root_copy(d, chip).wait_send()
        lat_copy(d).wait_send()

    each(1, chips, finish)
    each(0, chips, lambda d: pair_copy(d).wait_send())
    each(1, 2 * chips, lambda d: wave_copy(d, lat).wait_send())
    each(1, members, lambda d: thin_copy(d).wait_send())
    each(1, members // 2, lambda e: wide_copy(e, z).wait_send())
    half_copy.wait_send()


def transformed(waves, owner_map, band_widths, latitudes, owned, side):
    devices, per_device = waves.shape[:2]
    chips = devices // 2
    members = lax.axis_size("mem")
    half = LEVELS // 2
    dma = pltpu.SemaphoreType.DMA
    lanes = (MM + 127) // 128 * 128
    stride = (per_device + 7) // 8 * 8
    counts = [devices, chips, chips, members, members // 2, 1, chips, chips]
    return pl.pallas_call(
        functools.partial(band_kernel, side, chips, members),
        out_shape=(
            jax.ShapeDtypeStruct((2, owned, MM, LEVELS), jnp.bfloat16),
            jax.ShapeDtypeStruct((chips, LEVELS, LEVELS), jnp.float32),
        ),
        in_specs=[pl.BlockSpec(memory_space=pltpu.VMEM)] * 7,
        out_specs=(pl.BlockSpec(memory_space=pltpu.VMEM),) * 2,
        scratch_shapes=[
            pltpu.VMEM((MM, *latitudes[0].shape), jnp.float32),
            pltpu.VMEM(latitudes[0].shape, jnp.float32),
            pltpu.VMEM((chips * SLOTS, lanes), jnp.bfloat16),
            pltpu.VMEM((lanes, chips * SLOTS), jnp.bfloat16),
            pltpu.VMEM(waves.shape, jnp.bfloat16),
            pltpu.VMEM(((devices + 1) * stride, LEVELS), jnp.float32),
            pltpu.VMEM((owned, chips * SLOTS, 2 * LEVELS), jnp.bfloat16),
            pltpu.VMEM((owned, chips * SLOTS, 2 * LEVELS), jnp.bfloat16),
            pltpu.VMEM((chips, LEVELS, LEVELS), jnp.float32),
            pltpu.VMEM((chips, half, LEVELS), jnp.float32),
            pltpu.VMEM((chips, half, LEVELS), jnp.float32),
            pltpu.VMEM((chips, half, LEVELS), jnp.float32),
            pltpu.VMEM((half, LEVELS), jnp.float32),
            pltpu.VMEM((members, 8, LEVELS), jnp.float32),
            pltpu.VMEM((LEVELS, LEVELS), jnp.float32),
        ]
        + [dma((count,)) for count in counts for way in range(2)],
        compiler_params=pltpu.CompilerParams(
            collective_id=0, has_side_effects=True, vmem_limit_bytes=48 * 2**20
        ),
    )(waves, owner_map[None], band_widths[None], *latitudes)


def body(perturbation, owner_map, band_widths):
    lat_rows = perturbation.shape[1]
    lat_devices = lax.axis_size("lat")
    owned = MM // lat_devices
    wave_table = fourier_table(owner_map, NLON).reshape(2, lat_devices, owned, NLON)
    waves = jnp.einsum(
        "rdqk,jkl->drqjl", wave_table, perturbation[0], preferred_element_type=jnp.float32
    ).astype(jnp.bfloat16)
    waves = waves.reshape(lat_devices, 2 * owned * lat_rows, LEVELS)
    latitudes = latitude_rows(lat_rows * lat_devices, lat_rows)
    whitened, inverse_root = transformed(
        waves, owner_map, band_widths, latitudes, owned, CHIP_SIDE
    )
    return (whitened[None], inverse_root)


def solution(mesh):
    in_specs = (P("mem", "lat", None, None), P(), P())
    out_specs = (P("mem", None, "lat", None, None), P())
    return jax.shard_map(body, mesh=mesh, in_specs=in_specs, out_specs=out_specs, check_vma=False)
```
